128 devices in a mesh: row: 64 (over z, y, x), col: 2 (over core).
Axes of the slice: x: 4, y: 4, z: 4, core: 2. Of those that a mesh axis runs over, the one named last changes fastest.
Arguments:
- slab: bfloat16 [262144, 2048], P('row', 'col'), may hold values from -6 to 6
- gauss: bfloat16 [2048, 1024], P('col'), may hold values from -0.125 to 0.125
- pivots: int32 [1024], replicated, may hold values from 0 to 262143, as said below
- block_inverses: float32 [8, 128, 128], replicated, may hold values from -2 to 2
Outputs:
- factor_rows: float32 [262144, 1024], P(('row', 'col'))
- pivot_block: float32 [1024, 1024], P(('row', 'col'))
The draws below stay inside these ranges and needn't reach their ends.
Inputs may be any that keep to these rules, and one draw needn't show every extreme that they name: `pivots`: distinct row numbers; each aligned block of 2048 rows holds at most 32 of them, and some block holds exactly 32.
All inputs are finite; a program needn't handle non-finite values.
Results may differ from the reference program's by a relative error of at most 0.0003.
Values may be sent and summed in bfloat16 or wider, within the bound.
A program may use at most 128 MiB of HBM per device.

```python
import jax
import jax.numpy as jnp
import numpy as np
from jax import lax

K = 1024
SLAB = 2048
BLK = 128
NROWS = 262144
SHARD_ROWS = 2048
PIV_MOST = 32


def draw_pivots(key, part):
    blocks = NROWS // SHARD_ROWS
    remain = K - PIV_MOST
    base = remain // (blocks - 1)
    extra = remain - base * (blocks - 1)
    pattern = np.array([PIV_MOST] + [base + 1] * extra + [base] * (blocks - 1 - extra), dtype=np.int32)
    key_order = jax.random.fold_in(key, 11)
    key_rank = jax.random.fold_in(key, 12)
    key_shuffle = jax.random.fold_in(key, 13)
    order = jax.random.permutation(key_order, blocks)
    counts = jnp.asarray(pattern)[order]
    scores = jax.random.randint(key_rank, (blocks, SHARD_ROWS), 0, 1 << 20) * SHARD_ROWS + jnp.arange(SHARD_ROWS, dtype=jnp.int32)[None, :]
    ranks = jnp.argsort(jnp.argsort(scores, axis=1, stable=True), axis=1, stable=True)
    chosen = (ranks < counts[:, None]).reshape(-1)
    picked = jnp.nonzero(chosen, size=K, fill_value=0)[0].astype(jnp.int32)
    shuffle = jax.random.permutation(key_shuffle, K)
    return picked[shuffle].astype(jnp.int32)


def draw_block_inverses(key, part):
    count = K // BLK
    key_diag = jax.random.fold_in(key, 21)
    key_off = jax.random.fold_in(key, 22)
    diag = jax.random.uniform(key_diag, (count, BLK), jnp.float32, 0.6, 1.4)
    off = jax.random.normal(key_off, (count, BLK, BLK), jnp.float32) * (0.6 / BLK ** 0.5)
    rows = jnp.arange(BLK)[:, None]
    cols = jnp.arange(BLK)[None, :]
    upper = jnp.where(cols > rows, off, 0.0)
    eye = jnp.where(cols == rows, 1.0, 0.0)
    return (upper + diag[:, :, None] * eye[None, :, :]).astype(jnp.float32)


def level_of(key, dims, pieces, least, high):
    factor_of = 1.0
    for dim, blocks in pieces:
        heights = jax.random.uniform(jax.random.fold_in(jax.random.fold_in(key, 6), dim), (blocks,), jnp.float32, least / len(pieces), high / len(pieces))
        factor_of = factor_of * jnp.repeat(jnp.exp(heights), dims[dim] // blocks).reshape((-1,) + (1,) * (len(dims) - 1 - dim))
    return factor_of


def noise(key, dims, deviation, reach, cuts=(), kind=jnp.bfloat16):
    values = jax.random.normal(key, dims, jnp.float32) * deviation
    if len(cuts) > 0:
        values = level_of(key, dims, cuts, -0.22, 0.18) * values
    return jnp.clip(values, min=-reach, max=reach).astype(kind)


def setup_inputs(seed: int = 0) -> dict:
    arg_keys = jax.random.split(jax.random.key(seed), 5)
    return {
        "slab": noise(arg_keys[0], (NROWS, SLAB), 1.0, 6.0, ((0, 64), (1, 2))),
        "gauss": noise(arg_keys[1], (SLAB, K), SLAB ** -0.5, 0.125, ((0, 2),)),
        "pivots": draw_pivots(jax.random.fold_in(arg_keys[4], 71), 0),
        "block_inverses": draw_block_inverses(jax.random.fold_in(arg_keys[4], 71), 0),
    }


def reference(slab, gauss, pivots, block_inverses):
    sketch = jnp.dot(slab, gauss, preferred_element_type=jnp.float32)
    pivot_block = jnp.take(sketch, pivots, axis=0)
    factor = 1.0 / (K ** 0.5)
    solved = []
    for block in range(K // BLK):
        acc = sketch[:, block * BLK:(block + 1) * BLK]
        if block > 0:
            earlier = jnp.concatenate(solved, axis=1)
            coupling = pivot_block[:block * BLK, block * BLK:(block + 1) * BLK]
            acc = acc - factor * jnp.dot(earlier, coupling, precision=lax.Precision.HIGHEST)
        solved.append(jnp.dot(acc, block_inverses[block], precision=lax.Precision.HIGHEST))
    return jnp.concatenate(solved, axis=1), pivot_block
```

```python
import jax
import jax.numpy as jnp
from jax import lax
from jax.sharding import PartitionSpec as P

K = 1024
BLK = 128
SLOTS = 32


def on_device(slab, gauss, pivots, block_inverses):
    col_count = lax.axis_size("col")
    devices = lax.axis_size("row") * col_count
    col = lax.axis_index("col")
    owner = lax.axis_index("row") * col_count + col
    shard_rows = slab.shape[0] // col_count
    width = gauss.shape[1]
    swap = [(0, 1), (1, 0)]

    mine = lax.dynamic_slice_in_dim(slab, col * shard_rows, shard_rows, 0)
    theirs = lax.dynamic_slice_in_dim(slab, (1 - col) * shard_rows, shard_rows, 0)

    block_of = pivots // shard_rows
    onehot = block_of[:, None] == jnp.arange(devices, dtype=pivots.dtype)[None, :]
    rank = jnp.take_along_axis(jnp.cumsum(onehot.astype(jnp.int32), axis=0), block_of[:, None], axis=1)[:, 0] - 1
    local = pivots - block_of * shard_rows

    def slot_rows(b):
        hit = block_of == b
        return jnp.zeros((SLOTS,), jnp.int32).at[jnp.where(hit, rank, SLOTS)].set(local, mode="drop")

    partner = owner + 1 - 2 * col
    own_part = jnp.dot(jnp.take(mine, slot_rows(owner), axis=0), gauss, preferred_element_type=jnp.float32)
    for_partner = jnp.dot(jnp.take(theirs, slot_rows(partner), axis=0), gauss, preferred_element_type=jnp.float32)
    own_slots = own_part + lax.ppermute(for_partner, "col", swap)
    slots = lax.all_gather(own_slots, ("row", "col"), tiled=True)

    other_slab = lax.ppermute(theirs, "col", swap)
    other_gauss = lax.ppermute(gauss, "col", swap)
    sketch = jnp.dot(mine, gauss, preferred_element_type=jnp.float32) + jnp.dot(
        other_slab, other_gauss, preferred_element_type=jnp.float32
    )

    pivot_block = jnp.take(slots, block_of * SLOTS + rank, axis=0)
    share = width // devices
    own_pivots = lax.dynamic_slice_in_dim(pivot_block, owner * share, share, 0)

    factor = 1.0 / K**0.5
    solved = []
    for block in range(K // BLK):
        acc = sketch[:, block * BLK : (block + 1) * BLK]
        for earlier in range(block):
            coupling = pivot_block[earlier * BLK : (earlier + 1) * BLK, block * BLK : (block + 1) * BLK]
            acc = acc - factor * jnp.dot(solved[earlier], coupling, precision=lax.Precision.HIGH)
        solved.append(jnp.dot(acc, block_inverses[block], precision=lax.Precision.HIGH))
    factor_rows = jnp.concatenate(solved, axis=1)
    return (factor_rows, own_pivots)


def solution(mesh):
    return jax.shard_map(
        on_device,
        mesh=mesh,
        in_specs=(P("row", "col"), P("col", None), P(), P()),
        out_specs=(P(("row", "col"), None), P(("row", "col"), None)),
        check_vma=False,
    )
```

```python
import functools

import jax
import jax.numpy as jnp
from jax import lax
from jax.experimental import pallas as pl
from jax.experimental.pallas import tpu as pltpu
from jax.sharding import PartitionSpec as P

K = 1024
BLK = 128
SLOTS = 32
TM = 1024


def split(x):
    hi = x.astype(jnp.bfloat16)
    return hi, (x - hi.astype(jnp.float32)).astype(jnp.bfloat16)


def solve_kernel(factor, s_ref, p_ref, b_ref, f_ref, pcat, bcat, g):
    nb = s_ref.shape[1] // BLK

    @pl.when(pl.program_id(0) == 0)
    def _():
        for i in range(nb):
            hi, lo = split(p_ref[i * BLK:(i + 1) * BLK, :] * factor)
            pcat[3 * i * BLK:(3 * i + 1) * BLK, :] = hi
            pcat[(3 * i + 1) * BLK:(3 * i + 2) * BLK, :] = lo
            pcat[(3 * i + 2) * BLK:(3 * i + 3) * BLK, :] = hi
            bh, bl = split(b_ref[i])
            bcat[i, 0:BLK, :] = bh
            bcat[i, BLK:2 * BLK, :] = bl
            bcat[i, 2 * BLK:3 * BLK, :] = bh
    for j in range(nb):
        cols = slice(j * BLK, (j + 1) * BLK)
        acc = s_ref[:, cols]
        if j > 0:
            acc = acc - jnp.dot(g[:, : 3 * j * BLK], pcat[: 3 * j * BLK, cols], preferred_element_type=jnp.float32)
        a_hi, a_lo = split(acc)
        out = jnp.dot(jnp.concatenate([a_hi, a_hi, a_lo], axis=1), bcat[j], preferred_element_type=jnp.float32)
        f_ref[:, cols] = out
        if j + 1 < nb:
            o_hi, o_lo = split(out)
            g[:, 3 * j * BLK:(3 * j + 1) * BLK] = o_hi
            g[:, (3 * j + 1) * BLK:(3 * j + 2) * BLK] = o_hi
            g[:, (3 * j + 2) * BLK:(3 * j + 3) * BLK] = o_lo


def solve(sketch, pivot_block, block_inverses):
    rows, k = sketch.shape
    nb = k // BLK
    full = lambda shape: pl.BlockSpec(shape, lambda i: (0,) * len(shape))
    return pl.pallas_call(
        functools.partial(solve_kernel, 1.0 / k**0.5),
        out_shape=jax.ShapeDtypeStruct((rows, k), jnp.float32),
        grid=(rows // TM,),
        in_specs=[pl.BlockSpec((TM, k), lambda i: (i, 0)), full((k, k)), full(block_inverses.shape)],
        out_specs=pl.BlockSpec((TM, k), lambda i: (i, 0)),
        scratch_shapes=[pltpu.VMEM((3 * k, k), jnp.bfloat16), pltpu.VMEM((nb, 3 * BLK, BLK), jnp.bfloat16), pltpu.VMEM((TM, 3 * k), jnp.bfloat16)],
        compiler_params=pltpu.CompilerParams(vmem_limit_bytes=48 * 1024 * 1024),
    )(sketch, pivot_block, block_inverses)


def on_device(slab, gauss, pivots, block_inverses):
    col_count = lax.axis_size("col")
    devices = lax.axis_size("row") * col_count
    col = lax.axis_index("col")
    owner = lax.axis_index("row") * col_count + col
    shard_rows = slab.shape[0] // col_count
    width = gauss.shape[1]
    swap = [(0, 1), (1, 0)]

    order = jnp.arange(pivots.shape[0], dtype=jnp.int32)
    block_of = pivots // shard_rows
    same = (block_of[:, None] == block_of[None, :]) & (order[None, :] < order[:, None])
    rank = jnp.sum(same.astype(jnp.int32), axis=1)
    local = pivots - block_of * shard_rows
    partner = owner + 1 - 2 * col
    targets = jnp.concatenate([jnp.full((SLOTS,), owner), jnp.full((SLOTS,), partner)])
    offsets = jnp.concatenate([jnp.full((SLOTS,), col), jnp.full((SLOTS,), 1 - col)]) * shard_rows
    slot_ids = jnp.concatenate([jnp.arange(SLOTS), jnp.arange(SLOTS)])
    hit = (block_of[None, :] == targets[:, None]) & (rank[None, :] == slot_ids[:, None])
    valid = jnp.any(hit, axis=1)
    where_row = jnp.sum(jnp.where(hit, local[None, :], 0), axis=1) + offsets
    pick = (where_row[:, None] == jnp.arange(slab.shape[0], dtype=jnp.int32)[None, :]) & valid[:, None]
    rows = jnp.dot(pick.astype(slab.dtype), slab, preferred_element_type=jnp.float32).astype(slab.dtype)
    parts = jnp.dot(rows, gauss, preferred_element_type=jnp.float32)
    own_slots = parts[:SLOTS] + lax.ppermute(parts[SLOTS:], "col", swap)
    slots = lax.all_gather(own_slots, ("row", "col"), tiled=True)

    mine = lax.dynamic_slice_in_dim(slab, col * shard_rows, shard_rows, 0)
    theirs = lax.dynamic_slice_in_dim(slab, (1 - col) * shard_rows, shard_rows, 0)
    other_slab = lax.ppermute(theirs, "col", swap)
    other_gauss = lax.ppermute(gauss, "col", swap)
    sketch = jnp.dot(mine, gauss, preferred_element_type=jnp.float32) + jnp.dot(
        other_slab, other_gauss, preferred_element_type=jnp.float32
    )

    pivot_block = jnp.take(slots, block_of * SLOTS + rank, axis=0)
    share = width // devices
    own_pivots = lax.dynamic_slice_in_dim(pivot_block, owner * share, share, 0)
    factor_rows = solve(sketch, pivot_block, block_inverses)
    return (factor_rows, own_pivots)


def solution(mesh):
    return jax.shard_map(
        on_device,
        mesh=mesh,
        in_specs=(P("row", "col"), P("col", None), P(), P()),
        out_specs=(P(("row", "col"), None), P(("row", "col"), None)),
        check_vma=False,
    )
```

```python
import functools

import jax
import jax.numpy as jnp
from jax import lax
from jax.experimental import pallas as pl
from jax.experimental.pallas import tpu as pltpu
from jax.sharding import PartitionSpec as P

K = 1024
BLK = 128
SLOTS = 32
TM = 1024


def split(x):
    hi = x.astype(jnp.bfloat16)
    return hi, (x - hi.astype(jnp.float32)).astype(jnp.bfloat16)

def solve_kernel(factor, share, idx_ref, own_ref, s_ref, slots_hbm, b_ref, f_ref, piv_ref, pbuf, pcat, bcat, g, sem):
    nb = s_ref.shape[1] // BLK
    k = pbuf.shape[0]

    @pl.when(pl.program_id(0) == 0)
    def _():
        def fetch(r, carry):
            pltpu.make_async_copy(slots_hbm.at[pl.ds(idx_ref[r], 1)], pbuf.at[pl.ds(r, 1)], sem).start()
            return carry

        lax.fori_loop(0, k, fetch, 0, unroll=8)
        pltpu.make_async_copy(slots_hbm.at[pl.ds(0, k)], pbuf, sem).wait()
        piv_ref[...] = pbuf[pl.ds(pl.multiple_of(own_ref[0] * share, share), share), :]
        for i in range(nb):
            hi, lo = split(pbuf[i * BLK:(i + 1) * BLK, :] * factor)
            pcat[3 * i * BLK:(3 * i + 1) * BLK, :] = hi
            pcat[(3 * i + 1) * BLK:(3 * i + 2) * BLK, :] = lo
            pcat[(3 * i + 2) * BLK:(3 * i + 3) * BLK, :] = hi
            bh, bl = split(b_ref[i])
            bcat[i, 0:BLK, :] = bh
            bcat[i, BLK:2 * BLK, :] = bl
            bcat[i, 2 * BLK:3 * BLK, :] = bh

    for j in range(nb):
        cols = slice(j * BLK, (j + 1) * BLK)
        acc = s_ref[:, cols]
        if j > 0:
            acc = acc - jnp.dot(g[:, : 3 * j * BLK], pcat[: 3 * j * BLK, cols], preferred_element_type=jnp.float32)
        a_hi, a_lo = split(acc)
        out = jnp.dot(jnp.concatenate([a_hi, a_hi, a_lo], axis=1), bcat[j], preferred_element_type=jnp.float32)
        f_ref[:, cols] = out
        if j + 1 < nb:
            o_hi, o_lo = split(out)
            g[:, 3 * j * BLK:(3 * j + 1) * BLK] = o_hi
            g[:, (3 * j + 1) * BLK:(3 * j + 2) * BLK] = o_hi
            g[:, (3 * j + 2) * BLK:(3 * j + 3) * BLK] = o_lo


def solve(sketch, slots, idx, owner, share, block_inverses):
    rows, k = sketch.shape
    nb = k // BLK
    full = lambda shape: pl.BlockSpec(shape, lambda i, *_: (0,) * len(shape))
    return pl.pallas_call(
        functools.partial(solve_kernel, 1.0 / k**0.5, share),
        out_shape=(jax.ShapeDtypeStruct((rows, k), jnp.float32), jax.ShapeDtypeStruct((share, k), jnp.float32)),
        grid_spec=pltpu.PrefetchScalarGridSpec(
            num_scalar_prefetch=2,
            grid=(rows // TM,),
            in_specs=[pl.BlockSpec((TM, k), lambda i, *_: (i, 0)), pl.BlockSpec(memory_space=pl.ANY), full(block_inverses.shape)],
            out_specs=[pl.BlockSpec((TM, k), lambda i, *_: (i, 0)), full((share, k))],
            scratch_shapes=[
                pltpu.VMEM((k, k), jnp.float32),
                pltpu.VMEM((3 * k, k), jnp.bfloat16),
                pltpu.VMEM((nb, 3 * BLK, BLK), jnp.bfloat16),
                pltpu.VMEM((TM, 3 * k), jnp.bfloat16),
                pltpu.SemaphoreType.DMA,
            ],
        ),
        compiler_params=pltpu.CompilerParams(vmem_limit_bytes=56 * 1024 * 1024),
    )(idx, owner, sketch, slots, block_inverses)


def on_device(slab, gauss, pivots, block_inverses):
    col_count = lax.axis_size("col")
    devices = lax.axis_size("row") * col_count
    col = lax.axis_index("col")
    owner = lax.axis_index("row") * col_count + col
    shard_rows = slab.shape[0] // col_count
    width = gauss.shape[1]
    swap = [(0, 1), (1, 0)]

    order = jnp.arange(pivots.shape[0], dtype=jnp.int32)
    block_of = pivots // shard_rows
    same = (block_of[:, None] == block_of[None, :]) & (order[None, :] < order[:, None])
    rank = jnp.sum(same.astype(jnp.int32), axis=1)
    local = pivots - block_of * shard_rows
    partner = owner + 1 - 2 * col
    targets = jnp.concatenate([jnp.full((SLOTS,), owner), jnp.full((SLOTS,), partner)])
    offsets = jnp.concatenate([jnp.full((SLOTS,), col), jnp.full((SLOTS,), 1 - col)]) * shard_rows
    slot_ids = jnp.concatenate([jnp.arange(SLOTS), jnp.arange(SLOTS)])
    hit = (block_of[None, :] == targets[:, None]) & (rank[None, :] == slot_ids[:, None])
    valid = jnp.any(hit, axis=1)
    where_row = jnp.sum(jnp.where(hit, local[None, :], 0), axis=1) + offsets
    pick = (where_row[:, None] == jnp.arange(slab.shape[0], dtype=jnp.int32)[None, :]) & valid[:, None]
    rows = jnp.dot(pick.astype(slab.dtype), slab, preferred_element_type=jnp.float32).astype(slab.dtype)
    parts = jnp.dot(rows, gauss, preferred_element_type=jnp.float32)
    own_slots = parts[:SLOTS] + lax.ppermute(parts[SLOTS:], "col", swap)
    slots = lax.all_gather(own_slots, ("row", "col"), tiled=True)

    mine = lax.dynamic_slice_in_dim(slab, col * shard_rows, shard_rows, 0)
    theirs = lax.dynamic_slice_in_dim(slab, (1 - col) * shard_rows, shard_rows, 0)
    other_slab = lax.ppermute(theirs, "col", swap)
    other_gauss = lax.ppermute(gauss, "col", swap)
    sketch = jnp.dot(mine, gauss, preferred_element_type=jnp.float32) + jnp.dot(
        other_slab, other_gauss, preferred_element_type=jnp.float32
    )

    share = width // devices
    factor_rows, own_pivots = solve(sketch, slots, block_of * SLOTS + rank, owner[None], share, block_inverses)
    return (factor_rows, own_pivots)


def solution(mesh):
    return jax.shard_map(
        on_device,
        mesh=mesh,
        in_specs=(P("row", "col"), P("col", None), P(), P()),
        out_specs=(P(("row", "col"), None), P(("row", "col"), None)),
        check_vma=False,
    )
```

```python
import functools

import jax
import jax.numpy as jnp
from jax import lax
from jax.experimental import pallas as pl
from jax.experimental.pallas import tpu as pltpu
from jax.sharding import PartitionSpec as P

K = 1024
BLK = 128
SLOTS = 32
TM = 1024


def split(x):
    hi = x.astype(jnp.bfloat16)
    return hi, (x - hi.astype(jnp.float32)).astype(jnp.bfloat16)

def dot3(a, b):
    a_hi, a_lo = split(a)
    b_hi, b_lo = split(b)
    d = functools.partial(jnp.dot, preferred_element_type=jnp.float32)
    return d(a_hi, b_hi) + (d(a_hi, b_lo) + d(a_lo, b_hi))


def solve_kernel(factor, share, idx_ref, own_ref, s_ref, slots_hbm, b_ref, f_ref, piv_ref, pbuf, pcat, tcat, g, sem):
    nb = s_ref.shape[1] // BLK
    k = pbuf.shape[0]
    pw = 2 * BLK

    @pl.when(pl.program_id(0) == 0)
    def _():
        def fetch(r, carry):
            pltpu.make_async_copy(slots_hbm.at[pl.ds(idx_ref[r], 1)], pbuf.at[pl.ds(r, 1)], sem).start()
            return carry

        lax.fori_loop(0, k, fetch, 0, unroll=8)
        pltpu.make_async_copy(slots_hbm.at[pl.ds(0, k)], pbuf, sem).wait()
        piv_ref[...] = pbuf[pl.ds(pl.multiple_of(own_ref[0] * share, share), share), :]
        for i in range(nb):
            hi, lo = split(pbuf[i * BLK:(i + 1) * BLK, :] * factor)
            pcat[3 * i * BLK:(3 * i + 1) * BLK, :] = hi
            pcat[(3 * i + 1) * BLK:(3 * i + 2) * BLK, :] = lo
            pcat[(3 * i + 2) * BLK:(3 * i + 3) * BLK, :] = hi
        for q in range(nb // 2):
            a, b = 2 * q, 2 * q + 1
            cross = -dot3(dot3(b_ref[a], pbuf[a * BLK:b * BLK, b * BLK:(b + 1) * BLK] * factor), b_ref[b])
            zero = jnp.zeros((BLK, BLK), jnp.float32)
            panel = jnp.concatenate(
                [jnp.concatenate([b_ref[a], cross], axis=1), jnp.concatenate([zero, b_ref[b]], axis=1)], axis=0
            )
            hi, lo = split(panel)
            tcat[q, 0:pw, :] = hi
            tcat[q, pw:2 * pw, :] = lo
            tcat[q, 2 * pw:3 * pw, :] = hi

    for q in range(nb // 2):
        cols = slice(q * pw, (q + 1) * pw)
        acc = s_ref[:, cols]
        if q > 0:
            acc = acc - jnp.dot(g[:, : 3 * q * pw], pcat[: 3 * q * pw, cols], preferred_element_type=jnp.float32)
        a_hi, a_lo = split(acc)
        out = jnp.dot(jnp.concatenate([a_hi, a_hi, a_lo], axis=1), tcat[q], preferred_element_type=jnp.float32)
        f_ref[:, cols] = out
        if q + 1 < nb // 2:
            o_hi, o_lo = split(out)
            for h in range(2):
                blk = 2 * q + h
                part = slice(h * BLK, (h + 1) * BLK)
                g[:, 3 * blk * BLK:(3 * blk + 1) * BLK] = o_hi[:, part]
                g[:, (3 * blk + 1) * BLK:(3 * blk + 2) * BLK] = o_hi[:, part]
                g[:, (3 * blk + 2) * BLK:(3 * blk + 3) * BLK] = o_lo[:, part]


def solve(sketch, slots, idx, owner, share, block_inverses):
    rows, k = sketch.shape
    nb = k // BLK
    full = lambda shape: pl.BlockSpec(shape, lambda i, *_: (0,) * len(shape))
    return pl.pallas_call(
        functools.partial(solve_kernel, 1.0 / k**0.5, share),
        out_shape=(jax.ShapeDtypeStruct((rows, k), jnp.float32), jax.ShapeDtypeStruct((share, k), jnp.float32)),
        grid_spec=pltpu.PrefetchScalarGridSpec(
            num_scalar_prefetch=2,
            grid=(rows // TM,),
            in_specs=[pl.BlockSpec((TM, k), lambda i, *_: (i, 0)), pl.BlockSpec(memory_space=pl.ANY), full(block_inverses.shape)],
            out_specs=[pl.BlockSpec((TM, k), lambda i, *_: (i, 0)), full((share, k))],
            scratch_shapes=[
                pltpu.VMEM((k, k), jnp.float32),
                pltpu.VMEM((3 * k, k), jnp.bfloat16),
                pltpu.VMEM((nb // 2, 6 * BLK, 2 * BLK), jnp.bfloat16),
                pltpu.VMEM((TM, 3 * k), jnp.bfloat16),
                pltpu.SemaphoreType.DMA,
            ],
        ),
        compiler_params=pltpu.CompilerParams(vmem_limit_bytes=56 * 1024 * 1024),
    )(idx, owner, sketch, slots, block_inverses)


def on_device(slab, gauss, pivots, block_inverses):
    col_count = lax.axis_size("col")
    devices = lax.axis_size("row") * col_count
    col = lax.axis_index("col")
    owner = lax.axis_index("row") * col_count + col
    shard_rows = slab.shape[0] // col_count
    width = gauss.shape[1]
    swap = [(0, 1), (1, 0)]

    order = jnp.arange(pivots.shape[0], dtype=jnp.int32)
    block_of = pivots // shard_rows
    same = (block_of[:, None] == block_of[None, :]) & (order[None, :] < order[:, None])
    rank = jnp.sum(same.astype(jnp.int32), axis=1)
    local = pivots - block_of * shard_rows
    partner = owner + 1 - 2 * col
    targets = jnp.concatenate([jnp.full((SLOTS,), owner), jnp.full((SLOTS,), partner)])
    offsets = jnp.concatenate([jnp.full((SLOTS,), col), jnp.full((SLOTS,), 1 - col)]) * shard_rows
    slot_ids = jnp.concatenate([jnp.arange(SLOTS), jnp.arange(SLOTS)])
    hit = (block_of[None, :] == targets[:, None]) & (rank[None, :] == slot_ids[:, None])
    valid = jnp.any(hit, axis=1)
    where_row = jnp.sum(jnp.where(hit, local[None, :], 0), axis=1) + offsets
    pick = (where_row[:, None] == jnp.arange(slab.shape[0], dtype=jnp.int32)[None, :]) & valid[:, None]
    rows = jnp.dot(pick.astype(slab.dtype), slab, preferred_element_type=jnp.float32).astype(slab.dtype)
    parts = jnp.dot(rows, gauss, preferred_element_type=jnp.float32)
    own_slots = parts[:SLOTS] + lax.ppermute(parts[SLOTS:], "col", swap)
    slots = lax.all_gather(own_slots, ("row", "col"), tiled=True)

    mine = lax.dynamic_slice_in_dim(slab, col * shard_rows, shard_rows, 0)
    theirs = lax.dynamic_slice_in_dim(slab, (1 - col) * shard_rows, shard_rows, 0)
    other_slab = lax.ppermute(theirs, "col", swap)
    other_gauss = lax.ppermute(gauss, "col", swap)
    sketch = jnp.dot(mine, gauss, preferred_element_type=jnp.float32) + jnp.dot(
        other_slab, other_gauss, preferred_element_type=jnp.float32
    )

    share = width // devices
    factor_rows, own_pivots = solve(sketch, slots, block_of * SLOTS + rank, owner[None], share, block_inverses)
    return (factor_rows, own_pivots)


def solution(mesh):
    return jax.shard_map(
        on_device,
        mesh=mesh,
        in_specs=(P("row", "col"), P("col", None), P(), P()),
        out_specs=(P(("row", "col"), None), P(("row", "col"), None)),
        check_vma=False,
    )
```

```python
import functools

import jax
import jax.numpy as jnp
from jax import lax
from jax.experimental import pallas as pl
from jax.experimental.pallas import tpu as pltpu
from jax.sharding import PartitionSpec as P

K = 1024
BLK = 128
SLOTS = 32
TM = 1024


def split(x):
    hi = x.astype(jnp.bfloat16)
    return hi, (x - hi.astype(jnp.float32)).astype(jnp.bfloat16)

def dot3(a, b):
    a_hi, a_lo = split(a)
    b_hi, b_lo = split(b)
    d = functools.partial(jnp.dot, preferred_element_type=jnp.float32)
    return d(a_hi, b_hi) + (d(a_hi, b_lo) + d(a_lo, b_hi))


def solve_kernel(factor, share, idx_ref, own_ref, s_ref, slots_hbm, b_ref, f_ref, piv_ref, pbuf, pcat, tcat, g, sem):
    nb = s_ref.shape[1] // BLK
    k = pbuf.shape[0]
    pw = 2 * BLK

    @pl.when(pl.program_id(0) == 0)
    def _():
        def fetch(r, carry):
            pltpu.make_async_copy(slots_hbm.at[pl.ds(idx_ref[r], 1)], pbuf.at[pl.ds(r, 1)], sem).start()
            return carry

        lax.fori_loop(0, k, fetch, 0, unroll=8)
        pltpu.make_async_copy(slots_hbm.at[pl.ds(0, k)], pbuf, sem).wait()
        piv_ref[...] = pbuf[pl.ds(pl.multiple_of(own_ref[0] * share, share), share), :]
        for i in range(nb):
            hi, lo = split(pbuf[i * BLK:(i + 1) * BLK, :] * factor)
            pcat[3 * i * BLK:(3 * i + 1) * BLK, :] = hi
            pcat[(3 * i + 1) * BLK:(3 * i + 2) * BLK, :] = lo
            pcat[(3 * i + 2) * BLK:(3 * i + 3) * BLK, :] = hi
        for q in range(nb // 2):
            a, b = 2 * q, 2 * q + 1
            cross = -dot3(dot3(b_ref[a], pbuf[a * BLK:b * BLK, b * BLK:(b + 1) * BLK] * factor), b_ref[b])
            zero = jnp.zeros((BLK, BLK), jnp.float32)
            panel = jnp.concatenate(
                [jnp.concatenate([b_ref[a], cross], axis=1), jnp.concatenate([zero, b_ref[b]], axis=1)], axis=0
            )
            hi, lo = split(panel)
            tcat[q, 0:pw, :] = hi
            tcat[q, pw:2 * pw, :] = lo
            tcat[q, 2 * pw:3 * pw, :] = hi

    for q in range(nb // 2):
        cols = slice(q * pw, (q + 1) * pw)
        acc = s_ref[:, cols]
        if q > 0:
            acc = acc - jnp.dot(g[:, : 3 * q * pw], pcat[: 3 * q * pw, cols], preferred_element_type=jnp.float32)
        a_hi, a_lo = split(acc)
        out = jnp.dot(jnp.concatenate([a_hi, a_hi, a_lo], axis=1), tcat[q], preferred_element_type=jnp.float32)
        f_ref[:, cols] = out
        if q + 1 < nb // 2:
            o_hi, o_lo = split(out)
            for h in range(2):
                blk = 2 * q + h
                part = slice(h * BLK, (h + 1) * BLK)
                g[:, 3 * blk * BLK:(3 * blk + 1) * BLK] = o_hi[:, part]
                g[:, (3 * blk + 1) * BLK:(3 * blk + 2) * BLK] = o_hi[:, part]
                g[:, (3 * blk + 2) * BLK:(3 * blk + 3) * BLK] = o_lo[:, part]


def solve(sketch, slots, idx, owner, share, block_inverses):
    rows, k = sketch.shape
    nb = k // BLK
    full = lambda shape: pl.BlockSpec(shape, lambda i, *_: (0,) * len(shape))
    return pl.pallas_call(
        functools.partial(solve_kernel, 1.0 / k**0.5, share),
        out_shape=(jax.ShapeDtypeStruct((rows, k), jnp.float32), jax.ShapeDtypeStruct((share, k), jnp.float32)),
        grid_spec=pltpu.PrefetchScalarGridSpec(
            num_scalar_prefetch=2,
            grid=(rows // TM,),
            in_specs=[pl.BlockSpec((TM, k), lambda i, *_: (i, 0)), pl.BlockSpec(memory_space=pl.ANY), full(block_inverses.shape)],
            out_specs=[pl.BlockSpec((TM, k), lambda i, *_: (i, 0)), full((share, k))],
            scratch_shapes=[
                pltpu.VMEM((k, k), jnp.float32),
                pltpu.VMEM((3 * k, k), jnp.bfloat16),
                pltpu.VMEM((nb // 2, 6 * BLK, 2 * BLK), jnp.bfloat16),
                pltpu.VMEM((TM, 3 * k), jnp.bfloat16),
                pltpu.SemaphoreType.DMA,
            ],
        ),
        compiler_params=pltpu.CompilerParams(vmem_limit_bytes=56 * 1024 * 1024),
    )(idx, owner, sketch, slots, block_inverses)


def exchange_kernel(slab_hbm, gauss_hbm, slab_out, gauss_out, sems):
    row = lax.axis_index("row")
    partner = 1 - lax.axis_index("col")
    mesh_ids = pl.DeviceIdType.MESH
    barrier = pltpu.get_barrier_semaphore()
    pl.semaphore_signal(barrier, 1, device_id=(row, partner), device_id_type=mesh_ids)
    pl.semaphore_wait(barrier, 1)
    rows = slab_out.shape[0]
    copies = [
        pltpu.make_async_remote_copy(
            src_ref=slab_hbm.at[pl.ds(pl.multiple_of(partner * rows, rows), rows)],
            dst_ref=slab_out,
            send_sem=sems.at[0],
            recv_sem=sems.at[1],
            device_id=(row, partner),
            device_id_type=mesh_ids,
        ),
        pltpu.make_async_remote_copy(
            src_ref=gauss_hbm,
            dst_ref=gauss_out,
            send_sem=sems.at[2],
            recv_sem=sems.at[3],
            device_id=(row, partner),
            device_id_type=mesh_ids,
        ),
    ]
    for copy in copies:
        copy.start()
    for copy in copies:
        copy.wait()


def exchange(slab, gauss, rows):
    anywhere = pl.BlockSpec(memory_space=pl.ANY)
    return pl.pallas_call(
        exchange_kernel,
        out_shape=(jax.ShapeDtypeStruct((rows, slab.shape[1]), slab.dtype), jax.ShapeDtypeStruct(gauss.shape, gauss.dtype)),
        in_specs=[anywhere, anywhere],
        out_specs=[anywhere, anywhere],
        scratch_shapes=[pltpu.SemaphoreType.DMA((4,))],
        compiler_params=pltpu.CompilerParams(collective_id=0, has_side_effects=True),
    )(slab, gauss)


def on_device(slab, gauss, pivots, block_inverses):
    col_count = lax.axis_size("col")
    devices = lax.axis_size("row") * col_count
    col = lax.axis_index("col")
    owner = lax.axis_index("row") * col_count + col
    shard_rows = slab.shape[0] // col_count
    width = gauss.shape[1]
    swap = [(0, 1), (1, 0)]

    order = jnp.arange(pivots.shape[0], dtype=jnp.int32)
    block_of = pivots // shard_rows
    same = (block_of[:, None] == block_of[None, :]) & (order[None, :] < order[:, None])
    rank = jnp.sum(same.astype(jnp.int32), axis=1)
    local = pivots - block_of * shard_rows
    partner = owner + 1 - 2 * col
    targets = jnp.concatenate([jnp.full((SLOTS,), owner), jnp.full((SLOTS,), partner)])
    offsets = jnp.concatenate([jnp.full((SLOTS,), col), jnp.full((SLOTS,), 1 - col)]) * shard_rows
    slot_ids = jnp.concatenate([jnp.arange(SLOTS), jnp.arange(SLOTS)])
    hit = (block_of[None, :] == targets[:, None]) & (rank[None, :] == slot_ids[:, None])
    where_row = jnp.sum(jnp.where(hit, local[None, :], 0), axis=1) + offsets
    rows = jnp.take(slab, where_row, axis=0, mode="clip")
    parts = jnp.dot(rows, gauss, preferred_element_type=jnp.float32)
    own_slots = parts[:SLOTS] + lax.ppermute(parts[SLOTS:], "col", swap)
    slots = lax.all_gather(own_slots, ("row", "col"), tiled=True)

    mine = lax.dynamic_slice_in_dim(slab, col * shard_rows, shard_rows, 0)
    other_slab, other_gauss = exchange(slab, gauss, shard_rows)
    sketch = jnp.dot(mine, gauss, preferred_element_type=jnp.float32) + jnp.dot(
        other_slab, other_gauss, preferred_element_type=jnp.float32
    )

    share = width // devices
    factor_rows, own_pivots = solve(sketch, slots, block_of * SLOTS + rank, owner[None], share, block_inverses)
    return (factor_rows, own_pivots)


def solution(mesh):
    return jax.shard_map(
        on_device,
        mesh=mesh,
        in_specs=(P("row", "col"), P("col", None), P(), P()),
        out_specs=(P(("row", "col"), None), P(("row", "col"), None)),
        check_vma=False,
    )
```

```python
import functools

import jax
import jax.numpy as jnp
from jax import lax
from jax.experimental import pallas as pl
from jax.experimental.pallas import tpu as pltpu
from jax.sharding import PartitionSpec as P

K = 1024
BLK = 128
SLOTS = 32
TM = 1024


def split(x):
    hi = x.astype(jnp.bfloat16)
    return hi, (x - hi.astype(jnp.float32)).astype(jnp.bfloat16)


def dot3(a, b):
    a_hi, a_lo = split(a)
    b_hi, b_lo = split(b)
    d = functools.partial(jnp.dot, preferred_element_type=jnp.float32)
    return d(a_hi, b_hi) + (d(a_hi, b_lo) + d(a_lo, b_hi))


def put3(dst, row0, hi, lo, rows):
    dst[row0:row0 + rows] = hi
    dst[row0 + rows:row0 + 2 * rows] = lo
    dst[row0 + 2 * rows:row0 + 3 * rows] = hi


def scale_kernel(s_ref, b_ref, o_ref, dcat):
    nb = s_ref.shape[1] // BLK
    pw = 2 * BLK

    @pl.when(pl.program_id(0) == 0)
    def _():
        zero = jnp.zeros((BLK, BLK), jnp.float32)
        for q in range(nb // 2):
            a, b = 2 * q, 2 * q + 1
            panel = jnp.concatenate(
                [jnp.concatenate([b_ref[a], zero], axis=1), jnp.concatenate([zero, b_ref[b]], axis=1)], axis=0
            )
            hi, lo = split(panel)
            put3(dcat.at[q], 0, hi, lo, pw)

    for q in range(nb // 2):
        cols = slice(q * pw, (q + 1) * pw)
        a_hi, a_lo = split(s_ref[:, cols])
        o_ref[:, cols] = jnp.dot(jnp.concatenate([a_hi, a_hi, a_lo], axis=1), dcat[q], preferred_element_type=jnp.float32)


def scale(sketch, block_inverses):
    rows, k = sketch.shape
    full = lambda shape: pl.BlockSpec(shape, lambda i: (0,) * len(shape))
    return pl.pallas_call(
        scale_kernel,
        out_shape=jax.ShapeDtypeStruct((rows, k), jnp.float32),
        grid=(rows // TM,),
        in_specs=[pl.BlockSpec((TM, k), lambda i: (i, 0)), full(block_inverses.shape)],
        out_specs=pl.BlockSpec((TM, k), lambda i: (i, 0)),
        scratch_shapes=[pltpu.VMEM((k // BLK // 2, 6 * BLK, 2 * BLK), jnp.bfloat16)],
        compiler_params=pltpu.CompilerParams(vmem_limit_bytes=48 * 1024 * 1024),
    )(sketch, block_inverses)


def solve_kernel(factor, share, idx_ref, own_ref, s_ref, slots_hbm, b_ref, f_ref, piv_ref, pbuf, qcat, g, sem):
    nb = s_ref.shape[1] // BLK
    k = pbuf.shape[0]
    pw = 2 * BLK

    @pl.when(pl.program_id(0) == 0)
    def _():
        def fetch(r, carry):
            pltpu.make_async_copy(slots_hbm.at[pl.ds(idx_ref[r], 1)], pbuf.at[pl.ds(r, 1)], sem).start()
            return carry

        lax.fori_loop(0, k, fetch, 0, unroll=8)
        pltpu.make_async_copy(slots_hbm.at[pl.ds(0, k)], pbuf, sem).wait()
        piv_ref[...] = pbuf[pl.ds(pl.multiple_of(own_ref[0] * share, share), share), :]
        for j in range(1, nb):
            q = dot3(pbuf[: j * BLK, j * BLK:(j + 1) * BLK] * factor, b_ref[j])
            hi, lo = split(q)
            for i in range(j):
                put3(qcat.at[:, j * BLK:(j + 1) * BLK], 3 * i * BLK, hi[i * BLK:(i + 1) * BLK], lo[i * BLK:(i + 1) * BLK], BLK)

    for p in range(nb // 2):
        a, b = 2 * p, 2 * p + 1
        cols = slice(p * pw, (p + 1) * pw)
        acc = s_ref[:, cols]
        if p > 0:
            acc = acc - jnp.dot(g[:, : 3 * p * pw], qcat[: 3 * p * pw, cols], preferred_element_type=jnp.float32)
        f_a = acc[:, :BLK]
        a_hi, a_lo = split(f_a)
        f_b = acc[:, BLK:] - jnp.dot(
            jnp.concatenate([a_hi, a_hi, a_lo], axis=1), qcat[3 * a * BLK:3 * b * BLK, b * BLK:(b + 1) * BLK], preferred_element_type=jnp.float32
        )
        f_ref[:, a * BLK:b * BLK] = f_a
        f_ref[:, b * BLK:(b + 1) * BLK] = f_b
        if p + 1 < nb // 2:
            b_hi, b_lo = split(f_b)
            g[:, 3 * a * BLK:(3 * a + 1) * BLK] = a_hi
            g[:, (3 * a + 1) * BLK:(3 * a + 2) * BLK] = a_hi
            g[:, (3 * a + 2) * BLK:(3 * a + 3) * BLK] = a_lo
            g[:, 3 * b * BLK:(3 * b + 1) * BLK] = b_hi
            g[:, (3 * b + 1) * BLK:(3 * b + 2) * BLK] = b_hi
            g[:, (3 * b + 2) * BLK:(3 * b + 3) * BLK] = b_lo


def solve(sketch, slots, idx, owner, share, block_inverses):
    rows, k = sketch.shape
    full = lambda shape: pl.BlockSpec(shape, lambda i, *_: (0,) * len(shape))
    return pl.pallas_call(
        functools.partial(solve_kernel, 1.0 / k**0.5, share),
        out_shape=(jax.ShapeDtypeStruct((rows, k), jnp.float32), jax.ShapeDtypeStruct((share, k), jnp.float32)),
        grid_spec=pltpu.PrefetchScalarGridSpec(
            num_scalar_prefetch=2,
            grid=(rows // TM,),
            in_specs=[pl.BlockSpec((TM, k), lambda i, *_: (i, 0)), pl.BlockSpec(memory_space=pl.ANY), full(block_inverses.shape)],
            out_specs=[pl.BlockSpec((TM, k), lambda i, *_: (i, 0)), full((share, k))],
            scratch_shapes=[
                pltpu.VMEM((k, k), jnp.float32),
                pltpu.VMEM((3 * k, k), jnp.bfloat16),
                pltpu.VMEM((TM, 3 * k), jnp.bfloat16),
                pltpu.SemaphoreType.DMA,
            ],
        ),
        compiler_params=pltpu.CompilerParams(vmem_limit_bytes=56 * 1024 * 1024),
    )(idx, owner, sketch, slots, block_inverses)


def exchange_kernel(slab_hbm, gauss_hbm, slab_out, gauss_out, sems):
    row = lax.axis_index("row")
    partner = 1 - lax.axis_index("col")
    mesh_ids = pl.DeviceIdType.MESH
    barrier = pltpu.get_barrier_semaphore()
    pl.semaphore_signal(barrier, 1, device_id=(row, partner), device_id_type=mesh_ids)
    pl.semaphore_wait(barrier, 1)
    rows = slab_out.shape[0]
    copies = [
        pltpu.make_async_remote_copy(
            src_ref=slab_hbm.at[pl.ds(pl.multiple_of(partner * rows, rows), rows)],
            dst_ref=slab_out,
            send_sem=sems.at[0],
            recv_sem=sems.at[1],
            device_id=(row, partner),
            device_id_type=mesh_ids,
        ),
        pltpu.make_async_remote_copy(
            src_ref=gauss_hbm,
            dst_ref=gauss_out,
            send_sem=sems.at[2],
            recv_sem=sems.at[3],
            device_id=(row, partner),
            device_id_type=mesh_ids,
        ),
    ]
    for copy in copies:
        copy.start()
    for copy in copies:
        copy.wait()


def exchange(slab, gauss, rows):
    anywhere = pl.BlockSpec(memory_space=pl.ANY)
    return pl.pallas_call(
        exchange_kernel,
        out_shape=(jax.ShapeDtypeStruct((rows, slab.shape[1]), slab.dtype), jax.ShapeDtypeStruct(gauss.shape, gauss.dtype)),
        in_specs=[anywhere, anywhere],
        out_specs=[anywhere, anywhere],
        scratch_shapes=[pltpu.SemaphoreType.DMA((4,))],
        compiler_params=pltpu.CompilerParams(collective_id=0, has_side_effects=True),
    )(slab, gauss)


def on_device(slab, gauss, pivots, block_inverses):
    col_count = lax.axis_size("col")
    devices = lax.axis_size("row") * col_count
    col = lax.axis_index("col")
    owner = lax.axis_index("row") * col_count + col
    shard_rows = slab.shape[0] // col_count
    width = gauss.shape[1]
    swap = [(0, 1), (1, 0)]

    order = jnp.arange(pivots.shape[0], dtype=jnp.int32)
    block_of = pivots // shard_rows
    same = (block_of[:, None] == block_of[None, :]) & (order[None, :] < order[:, None])
    rank = jnp.sum(same.astype(jnp.int32), axis=1)
    local = pivots - block_of * shard_rows
    partner = owner + 1 - 2 * col
    targets = jnp.concatenate([jnp.full((SLOTS,), owner), jnp.full((SLOTS,), partner)])
    offsets = jnp.concatenate([jnp.full((SLOTS,), col), jnp.full((SLOTS,), 1 - col)]) * shard_rows
    slot_ids = jnp.concatenate([jnp.arange(SLOTS), jnp.arange(SLOTS)])
    hit = (block_of[None, :] == targets[:, None]) & (rank[None, :] == slot_ids[:, None])
    where_row = jnp.sum(jnp.where(hit, local[None, :], 0), axis=1) + offsets
    rows = jnp.take(slab, where_row, axis=0, mode="clip")
    parts = jnp.dot(rows, gauss, preferred_element_type=jnp.float32)
    own_slots = parts[:SLOTS] + lax.ppermute(parts[SLOTS:], "col", swap)
    slots = lax.all_gather(own_slots, ("row", "col"), tiled=True)

    mine = lax.dynamic_slice_in_dim(slab, col * shard_rows, shard_rows, 0)
    other_slab, other_gauss = exchange(slab, gauss, shard_rows)
    sketch = jnp.dot(mine, gauss, preferred_element_type=jnp.float32) + jnp.dot(
        other_slab, other_gauss, preferred_element_type=jnp.float32
    )

    share = width // devices
    scaled = scale(sketch, block_inverses)
    factor_rows, own_pivots = solve(scaled, slots, block_of * SLOTS + rank, owner[None], share, block_inverses)
    return (factor_rows, own_pivots)


def solution(mesh):
    return jax.shard_map(
        on_device,
        mesh=mesh,
        in_specs=(P("row", "col"), P("col", None), P(), P()),
        out_specs=(P(("row", "col"), None), P(("row", "col"), None)),
        check_vma=False,
    )
```

```python
import functools

import jax
import jax.numpy as jnp
from jax import lax
from jax.experimental import pallas as pl
from jax.experimental.pallas import tpu as pltpu
from jax.sharding import PartitionSpec as P

K = 1024
BLK = 128
SLOTS = 32
TM = 1024


def split(x):
    hi = x.astype(jnp.bfloat16)
    return hi, (x - hi.astype(jnp.float32)).astype(jnp.bfloat16)


def dot3(a, b):
    a_hi, a_lo = split(a)
    b_hi, b_lo = split(b)
    d = functools.partial(jnp.dot, preferred_element_type=jnp.float32)
    return d(a_hi, b_hi) + (d(a_hi, b_lo) + d(a_lo, b_hi))


def put3(dst, row0, hi, lo, rows):
    dst[row0:row0 + rows] = hi
    dst[row0 + rows:row0 + 2 * rows] = lo
    dst[row0 + 2 * rows:row0 + 3 * rows] = hi


def scale_kernel(s_ref, b_ref, o_ref, dcat):
    nb = s_ref.shape[1] // BLK
    pw = 2 * BLK

    @pl.when(pl.program_id(0) == 0)
    def _():
        zero = jnp.zeros((BLK, BLK), jnp.float32)
        for q in range(nb // 2):
            a, b = 2 * q, 2 * q + 1
            panel = jnp.concatenate(
                [jnp.concatenate([b_ref[a], zero], axis=1), jnp.concatenate([zero, b_ref[b]], axis=1)], axis=0
            )
            hi, lo = split(panel)
            put3(dcat.at[q], 0, hi, lo, pw)

    for q in range(nb // 2):
        cols = slice(q * pw, (q + 1) * pw)
        a_hi, a_lo = split(s_ref[:, cols])
        o_ref[:, cols] = jnp.dot(jnp.concatenate([a_hi, a_hi, a_lo], axis=1), dcat[q], preferred_element_type=jnp.float32)


def scale(sketch, block_inverses):
    rows, k = sketch.shape
    full = lambda shape: pl.BlockSpec(shape, lambda i: (0,) * len(shape))
    return pl.pallas_call(
        scale_kernel,
        out_shape=jax.ShapeDtypeStruct((rows, k), jnp.float32),
        grid=(rows // TM,),
        in_specs=[pl.BlockSpec((TM, k), lambda i: (i, 0)), full(block_inverses.shape)],
        out_specs=pl.BlockSpec((TM, k), lambda i: (i, 0)),
        scratch_shapes=[pltpu.VMEM((k // BLK // 2, 6 * BLK, 2 * BLK), jnp.bfloat16)],
        compiler_params=pltpu.CompilerParams(vmem_limit_bytes=48 * 1024 * 1024),
    )(sketch, block_inverses)


def solve_kernel(factor, share, idx_ref, own_ref, s_ref, slots_hbm, b_ref, f_ref, piv_ref, pbuf, qcat, g, sem):
    nb = s_ref.shape[1] // BLK
    k = pbuf.shape[0]
    pw = 2 * BLK

    @pl.when(pl.program_id(0) == 0)
    def _():
        used = k - BLK

        def fetch(r, carry):
            pltpu.make_async_copy(slots_hbm.at[pl.ds(idx_ref[r], 1)], pbuf.at[pl.ds(r, 1)], sem.at[0]).start()
            return carry

        lax.fori_loop(0, used, fetch, 0, unroll=8)
        first = own_ref[0] * share
        for r in range(share):
            pltpu.make_async_copy(slots_hbm.at[pl.ds(idx_ref[first + r], 1)], piv_ref.at[pl.ds(r, 1)], sem.at[1]).start()
        pltpu.make_async_copy(slots_hbm.at[pl.ds(0, used)], pbuf.at[pl.ds(0, used)], sem.at[0]).wait()
        pltpu.make_async_copy(slots_hbm.at[pl.ds(0, share)], piv_ref, sem.at[1]).wait()
        for j in range(1, nb):
            q = dot3(pbuf[: j * BLK, j * BLK:(j + 1) * BLK] * factor, b_ref[j])
            hi, lo = split(q)
            for i in range(j):
                put3(qcat.at[:, j * BLK:(j + 1) * BLK], 3 * i * BLK, hi[i * BLK:(i + 1) * BLK], lo[i * BLK:(i + 1) * BLK], BLK)

    for p in range(nb // 2):
        a, b = 2 * p, 2 * p + 1
        cols = slice(p * pw, (p + 1) * pw)
        acc = s_ref[:, cols]
        if p > 0:
            acc = acc - jnp.dot(g[:, : 3 * p * pw], qcat[: 3 * p * pw, cols], preferred_element_type=jnp.float32)
        f_a = acc[:, :BLK]
        a_hi, a_lo = split(f_a)
        f_b = acc[:, BLK:] - jnp.dot(
            jnp.concatenate([a_hi, a_hi, a_lo], axis=1), qcat[3 * a * BLK:3 * b * BLK, b * BLK:(b + 1) * BLK], preferred_element_type=jnp.float32
        )
        f_ref[:, a * BLK:b * BLK] = f_a
        f_ref[:, b * BLK:(b + 1) * BLK] = f_b
        if p + 1 < nb // 2:
            b_hi, b_lo = split(f_b)
            g[:, 3 * a * BLK:(3 * a + 1) * BLK] = a_hi
            g[:, (3 * a + 1) * BLK:(3 * a + 2) * BLK] = a_hi
            g[:, (3 * a + 2) * BLK:(3 * a + 3) * BLK] = a_lo
            g[:, 3 * b * BLK:(3 * b + 1) * BLK] = b_hi
            g[:, (3 * b + 1) * BLK:(3 * b + 2) * BLK] = b_hi
            g[:, (3 * b + 2) * BLK:(3 * b + 3) * BLK] = b_lo


def solve(sketch, slots, idx, owner, share, block_inverses):
    rows, k = sketch.shape
    full = lambda shape: pl.BlockSpec(shape, lambda i, *_: (0,) * len(shape))
    return pl.pallas_call(
        functools.partial(solve_kernel, 1.0 / k**0.5, share),
        out_shape=(jax.ShapeDtypeStruct((rows, k), jnp.float32), jax.ShapeDtypeStruct((share, k), jnp.float32)),
        grid_spec=pltpu.PrefetchScalarGridSpec(
            num_scalar_prefetch=2,
            grid=(rows // TM,),
            in_specs=[pl.BlockSpec((TM, k), lambda i, *_: (i, 0)), pl.BlockSpec(memory_space=pl.ANY), full(block_inverses.shape)],
            out_specs=[pl.BlockSpec((TM, k), lambda i, *_: (i, 0)), full((share, k))],
            scratch_shapes=[
                pltpu.VMEM((k, k), jnp.float32),
                pltpu.VMEM((3 * k, k), jnp.bfloat16),
                pltpu.VMEM((TM, 3 * k), jnp.bfloat16),
                pltpu.SemaphoreType.DMA((2,)),
            ],
        ),
        compiler_params=pltpu.CompilerParams(vmem_limit_bytes=56 * 1024 * 1024),
    )(idx, owner, sketch, slots, block_inverses)


def exchange_kernel(slab_hbm, gauss_hbm, slab_out, gauss_out, sems):
    row = lax.axis_index("row")
    partner = 1 - lax.axis_index("col")
    mesh_ids = pl.DeviceIdType.MESH
    barrier = pltpu.get_barrier_semaphore()
    pl.semaphore_signal(barrier, 1, device_id=(row, partner), device_id_type=mesh_ids)
    pl.semaphore_wait(barrier, 1)
    rows = slab_out.shape[0]
    copies = [
        pltpu.make_async_remote_copy(
            src_ref=slab_hbm.at[pl.ds(pl.multiple_of(partner * rows, rows), rows)],
            dst_ref=slab_out,
            send_sem=sems.at[0],
            recv_sem=sems.at[1],
            device_id=(row, partner),
            device_id_type=mesh_ids,
        ),
        pltpu.make_async_remote_copy(
            src_ref=gauss_hbm,
            dst_ref=gauss_out,
            send_sem=sems.at[2],
            recv_sem=sems.at[3],
            device_id=(row, partner),
            device_id_type=mesh_ids,
        ),
    ]
    for copy in copies:
        copy.start()
    for copy in copies:
        copy.wait()


def exchange(slab, gauss, rows):
    anywhere = pl.BlockSpec(memory_space=pl.ANY)
    return pl.pallas_call(
        exchange_kernel,
        out_shape=(jax.ShapeDtypeStruct((rows, slab.shape[1]), slab.dtype), jax.ShapeDtypeStruct(gauss.shape, gauss.dtype)),
        in_specs=[anywhere, anywhere],
        out_specs=[anywhere, anywhere],
        scratch_shapes=[pltpu.SemaphoreType.DMA((4,))],
        compiler_params=pltpu.CompilerParams(collective_id=0, has_side_effects=True),
    )(slab, gauss)


def on_device(slab, gauss, pivots, block_inverses):
    col_count = lax.axis_size("col")
    devices = lax.axis_size("row") * col_count
    col = lax.axis_index("col")
    owner = lax.axis_index("row") * col_count + col
    shard_rows = slab.shape[0] // col_count
    width = gauss.shape[1]
    swap = [(0, 1), (1, 0)]

    order = jnp.arange(pivots.shape[0], dtype=jnp.int32)
    block_of = pivots // shard_rows
    same = (block_of[:, None] == block_of[None, :]) & (order[None, :] < order[:, None])
    rank = jnp.sum(same.astype(jnp.int32), axis=1)
    local = pivots - block_of * shard_rows
    partner = owner + 1 - 2 * col
    targets = jnp.concatenate([jnp.full((SLOTS,), owner), jnp.full((SLOTS,), partner)])
    offsets = jnp.concatenate([jnp.full((SLOTS,), col), jnp.full((SLOTS,), 1 - col)]) * shard_rows
    slot_ids = jnp.concatenate([jnp.arange(SLOTS), jnp.arange(SLOTS)])
    hit = (block_of[None, :] == targets[:, None]) & (rank[None, :] == slot_ids[:, None])
    where_row = jnp.sum(jnp.where(hit, local[None, :], 0), axis=1) + offsets
    pick = where_row[:, None] == jnp.arange(slab.shape[0], dtype=jnp.int32)[None, :]
    rows = jnp.dot(pick.astype(slab.dtype), slab, preferred_element_type=jnp.float32).astype(slab.dtype)
    parts = jnp.dot(rows, gauss, preferred_element_type=jnp.float32)
    own_slots = parts[:SLOTS] + lax.ppermute(parts[SLOTS:], "col", swap)
    slots = lax.all_gather(own_slots, ("row", "col"), tiled=True)

    mine = lax.dynamic_slice_in_dim(slab, col * shard_rows, shard_rows, 0)
    other_slab, other_gauss = exchange(slab, gauss, shard_rows)
    sketch = jnp.dot(mine, gauss, preferred_element_type=jnp.float32) + jnp.dot(
        other_slab, other_gauss, preferred_element_type=jnp.float32
    )

    share = width // devices
    scaled = scale(sketch, block_inverses)
    factor_rows, own_pivots = solve(scaled, slots, block_of * SLOTS + rank, owner[None], share, block_inverses)
    return (factor_rows, own_pivots)


def solution(mesh):
    return jax.shard_map(
        on_device,
        mesh=mesh,
        in_specs=(P("row", "col"), P("col", None), P(), P()),
        out_specs=(P(("row", "col"), None), P(("row", "col"), None)),
        check_vma=False,
    )
```

```python
import functools

import jax
import jax.numpy as jnp
from jax import lax
from jax.experimental import pallas as pl
from jax.experimental.pallas import tpu as pltpu
from jax.sharding import PartitionSpec as P

K = 1024
BLK = 128
SLOTS = 32
GROUP = 16
TM = 1024


def split(x):
    hi = x.astype(jnp.bfloat16)
    return hi, (x - hi.astype(jnp.float32)).astype(jnp.bfloat16)


def dot3(a, b):
    a_hi, a_lo = split(a)
    b_hi, b_lo = split(b)
    d = functools.partial(jnp.dot, preferred_element_type=jnp.float32)
    return d(a_hi, b_hi) + (d(a_hi, b_lo) + d(a_lo, b_hi))


def put3(dst, row0, hi, lo, rows):
    dst[row0:row0 + rows] = hi
    dst[row0 + rows:row0 + 2 * rows] = lo
    dst[row0 + 2 * rows:row0 + 3 * rows] = hi


def scale_kernel(s_ref, b_ref, o_ref, dcat):
    nb = s_ref.shape[1] // BLK
    pw = 2 * BLK

    @pl.when(pl.program_id(0) == 0)
    def _():
        zero = jnp.zeros((BLK, BLK), jnp.float32)
        for q in range(nb // 2):
            a, b = 2 * q, 2 * q + 1
            panel = jnp.concatenate(
                [jnp.concatenate([b_ref[a], zero], axis=1), jnp.concatenate([zero, b_ref[b]], axis=1)], axis=0
            )
            hi, lo = split(panel)
            put3(dcat.at[q], 0, hi, lo, pw)

    for q in range(nb // 2):
        cols = slice(q * pw, (q + 1) * pw)
        a_hi, a_lo = split(s_ref[:, cols])
        o_ref[:, cols] = jnp.dot(jnp.concatenate([a_hi, a_hi, a_lo], axis=1), dcat[q], preferred_element_type=jnp.float32)


def scale(sketch, block_inverses):
    rows, k = sketch.shape
    full = lambda shape: pl.BlockSpec(shape, lambda i: (0,) * len(shape))
    return pl.pallas_call(
        scale_kernel,
        out_shape=jax.ShapeDtypeStruct((rows, k), jnp.float32),
        grid=(rows // TM,),
        in_specs=[pl.BlockSpec((TM, k), lambda i: (i, 0)), full(block_inverses.shape)],
        out_specs=pl.BlockSpec((TM, k), lambda i: (i, 0)),
        scratch_shapes=[pltpu.VMEM((k // BLK // 2, 6 * BLK, 2 * BLK), jnp.bfloat16)],
        compiler_params=pltpu.CompilerParams(vmem_limit_bytes=48 * 1024 * 1024),
    )(sketch, block_inverses)


def solve_kernel(factor, share, idx_ref, own_ref, s_ref, slots_hbm, b_ref, f_ref, piv_ref, pbuf, qcat, g, sem):
    nb = s_ref.shape[1] // BLK
    k = pbuf.shape[0]
    pw = 2 * BLK

    @pl.when(pl.program_id(0) == 0)
    def _():
        used = k - BLK

        def fetch(r, carry):
            pltpu.make_async_copy(slots_hbm.at[pl.ds(idx_ref[r], 1)], pbuf.at[pl.ds(r, 1)], sem.at[0]).start()
            return carry

        lax.fori_loop(0, used, fetch, 0, unroll=8)
        first = own_ref[0] * share
        for r in range(share):
            pltpu.make_async_copy(slots_hbm.at[pl.ds(idx_ref[first + r], 1)], piv_ref.at[pl.ds(r, 1)], sem.at[1]).start()
        pltpu.make_async_copy(slots_hbm.at[pl.ds(0, used)], pbuf.at[pl.ds(0, used)], sem.at[0]).wait()
        pltpu.make_async_copy(slots_hbm.at[pl.ds(0, share)], piv_ref, sem.at[1]).wait()
        for j in range(1, nb):
            q = dot3(pbuf[: j * BLK, j * BLK:(j + 1) * BLK] * factor, b_ref[j])
            hi, lo = split(q)
            for i in range(j):
                put3(qcat.at[:, j * BLK:(j + 1) * BLK], 3 * i * BLK, hi[i * BLK:(i + 1) * BLK], lo[i * BLK:(i + 1) * BLK], BLK)

    for p in range(nb // 2):
        a, b = 2 * p, 2 * p + 1
        cols = slice(p * pw, (p + 1) * pw)
        acc = s_ref[:, cols]
        if p > 0:
            acc = acc - jnp.dot(g[:, : 3 * p * pw], qcat[: 3 * p * pw, cols], preferred_element_type=jnp.float32)
        f_a = acc[:, :BLK]
        a_hi, a_lo = split(f_a)
        f_b = acc[:, BLK:] - jnp.dot(
            jnp.concatenate([a_hi, a_hi, a_lo], axis=1), qcat[3 * a * BLK:3 * b * BLK, b * BLK:(b + 1) * BLK], preferred_element_type=jnp.float32
        )
        f_ref[:, a * BLK:b * BLK] = f_a
        f_ref[:, b * BLK:(b + 1) * BLK] = f_b
        if p + 1 < nb // 2:
            b_hi, b_lo = split(f_b)
            g[:, 3 * a * BLK:(3 * a + 1) * BLK] = a_hi
            g[:, (3 * a + 1) * BLK:(3 * a + 2) * BLK] = a_hi
            g[:, (3 * a + 2) * BLK:(3 * a + 3) * BLK] = a_lo
            g[:, 3 * b * BLK:(3 * b + 1) * BLK] = b_hi
            g[:, (3 * b + 1) * BLK:(3 * b + 2) * BLK] = b_hi
            g[:, (3 * b + 2) * BLK:(3 * b + 3) * BLK] = b_lo


def solve(sketch, slots, idx, owner, share, block_inverses):
    rows, k = sketch.shape
    full = lambda shape: pl.BlockSpec(shape, lambda i, *_: (0,) * len(shape))
    return pl.pallas_call(
        functools.partial(solve_kernel, 1.0 / k**0.5, share),
        out_shape=(jax.ShapeDtypeStruct((rows, k), jnp.float32), jax.ShapeDtypeStruct((share, k), jnp.float32)),
        grid_spec=pltpu.PrefetchScalarGridSpec(
            num_scalar_prefetch=2,
            grid=(rows // TM,),
            in_specs=[pl.BlockSpec((TM, k), lambda i, *_: (i, 0)), pl.BlockSpec(memory_space=pl.ANY), full(block_inverses.shape)],
            out_specs=[pl.BlockSpec((TM, k), lambda i, *_: (i, 0)), full((share, k))],
            scratch_shapes=[
                pltpu.VMEM((k, k), jnp.float32),
                pltpu.VMEM((3 * k, k), jnp.bfloat16),
                pltpu.VMEM((TM, 3 * k), jnp.bfloat16),
                pltpu.SemaphoreType.DMA((2,)),
            ],
        ),
        compiler_params=pltpu.CompilerParams(vmem_limit_bytes=56 * 1024 * 1024),
    )(idx, owner, sketch, slots, block_inverses)


def pick_kernel(base_ref, within_ref, slab_hbm, gauss_hbm, out_ref, grp, gbuf, sems):
    n = within_ref.shape[0]
    load_gauss = pltpu.make_async_copy(gauss_hbm, gbuf, sems.at[0])
    load_gauss.start()
    for s in range(n):
        start = pl.multiple_of(base_ref[s] * GROUP, GROUP)
        pltpu.make_async_copy(slab_hbm.at[pl.ds(start, GROUP)], grp.at[pl.ds(s * GROUP, GROUP)], sems.at[1]).start()
    pltpu.make_async_copy(slab_hbm.at[pl.ds(0, n * GROUP)], grp, sems.at[1]).wait()
    target = lax.broadcasted_iota(jnp.int32, (n, n * GROUP), 0) * GROUP + within_ref[...]
    onehot = (lax.broadcasted_iota(jnp.int32, (n, n * GROUP), 1) == target).astype(grp.dtype)
    rows = jnp.dot(onehot, grp[...], preferred_element_type=jnp.float32).astype(grp.dtype)
    load_gauss.wait()
    out_ref[...] = jnp.dot(rows, gbuf[...], preferred_element_type=jnp.float32)


def pick(slab, gauss, where_row):
    n = where_row.shape[0]
    anywhere = pl.BlockSpec(memory_space=pl.ANY)
    return pl.pallas_call(
        pick_kernel,
        out_shape=jax.ShapeDtypeStruct((n, gauss.shape[1]), jnp.float32),
        in_specs=[pl.BlockSpec(memory_space=pltpu.SMEM), pl.BlockSpec(memory_space=pltpu.VMEM), anywhere, anywhere],
        out_specs=pl.BlockSpec(memory_space=pltpu.VMEM),
        scratch_shapes=[pltpu.VMEM((n * GROUP, slab.shape[1]), slab.dtype), pltpu.VMEM(gauss.shape, gauss.dtype), pltpu.SemaphoreType.DMA((2,))],
    )(where_row // GROUP, (where_row % GROUP)[:, None], slab, gauss)


def exchange_kernel(slab_hbm, gauss_hbm, slab_out, gauss_out, sems):
    row = lax.axis_index("row")
    partner = 1 - lax.axis_index("col")
    mesh_ids = pl.DeviceIdType.MESH
    barrier = pltpu.get_barrier_semaphore()
    pl.semaphore_signal(barrier, 1, device_id=(row, partner), device_id_type=mesh_ids)
    pl.semaphore_wait(barrier, 1)
    rows = slab_out.shape[0]
    copies = [
        pltpu.make_async_remote_copy(
            src_ref=slab_hbm.at[pl.ds(pl.multiple_of(partner * rows, rows), rows)],
            dst_ref=slab_out,
            send_sem=sems.at[0],
            recv_sem=sems.at[1],
            device_id=(row, partner),
            device_id_type=mesh_ids,
        ),
        pltpu.make_async_remote_copy(
            src_ref=gauss_hbm,
            dst_ref=gauss_out,
            send_sem=sems.at[2],
            recv_sem=sems.at[3],
            device_id=(row, partner),
            device_id_type=mesh_ids,
        ),
    ]
    for copy in copies:
        copy.start()
    for copy in copies:
        copy.wait()


def exchange(slab, gauss, rows):
    anywhere = pl.BlockSpec(memory_space=pl.ANY)
    return pl.pallas_call(
        exchange_kernel,
        out_shape=(jax.ShapeDtypeStruct((rows, slab.shape[1]), slab.dtype), jax.ShapeDtypeStruct(gauss.shape, gauss.dtype)),
        in_specs=[anywhere, anywhere],
        out_specs=[anywhere, anywhere],
        scratch_shapes=[pltpu.SemaphoreType.DMA((4,))],
        compiler_params=pltpu.CompilerParams(collective_id=0, has_side_effects=True),
    )(slab, gauss)


def on_device(slab, gauss, pivots, block_inverses):
    col_count = lax.axis_size("col")
    devices = lax.axis_size("row") * col_count
    col = lax.axis_index("col")
    owner = lax.axis_index("row") * col_count + col
    shard_rows = slab.shape[0] // col_count
    width = gauss.shape[1]
    swap = [(0, 1), (1, 0)]

    order = jnp.arange(pivots.shape[0], dtype=jnp.int32)
    block_of = pivots // shard_rows
    same = (block_of[:, None] == block_of[None, :]) & (order[None, :] < order[:, None])
    rank = jnp.sum(same.astype(jnp.int32), axis=1)
    local = pivots - block_of * shard_rows
    partner = owner + 1 - 2 * col
    targets = jnp.concatenate([jnp.full((SLOTS,), owner), jnp.full((SLOTS,), partner)])
    offsets = jnp.concatenate([jnp.full((SLOTS,), col), jnp.full((SLOTS,), 1 - col)]) * shard_rows
    slot_ids = jnp.concatenate([jnp.arange(SLOTS), jnp.arange(SLOTS)])
    hit = (block_of[None, :] == targets[:, None]) & (rank[None, :] == slot_ids[:, None])
    where_row = jnp.sum(jnp.where(hit, local[None, :], 0), axis=1) + offsets
    parts = pick(slab, gauss, where_row)
    own_slots = parts[:SLOTS] + lax.ppermute(parts[SLOTS:], "col", swap)
    slots = lax.all_gather(own_slots, ("row", "col"), tiled=True)

    mine = lax.dynamic_slice_in_dim(slab, col * shard_rows, shard_rows, 0)
    other_slab, other_gauss = exchange(slab, gauss, shard_rows)
    sketch = jnp.dot(mine, gauss, preferred_element_type=jnp.float32) + jnp.dot(
        other_slab, other_gauss, preferred_element_type=jnp.float32
    )

    share = width // devices
    scaled = scale(sketch, block_inverses)
    factor_rows, own_pivots = solve(scaled, slots, block_of * SLOTS + rank, owner[None], share, block_inverses)
    return (factor_rows, own_pivots)


def solution(mesh):
    return jax.shard_map(
        on_device,
        mesh=mesh,
        in_specs=(P("row", "col"), P("col", None), P(), P()),
        out_specs=(P(("row", "col"), None), P(("row", "col"), None)),
        check_vma=False,
    )
```

```python
import functools

import jax
import jax.numpy as jnp
from jax import lax
from jax.experimental import pallas as pl
from jax.experimental.pallas import tpu as pltpu
from jax.sharding import PartitionSpec as P

K = 1024
BLK = 128
SLOTS = 32
TM = 1024


def split(x):
    hi = x.astype(jnp.bfloat16)
    return hi, (x - hi.astype(jnp.float32)).astype(jnp.bfloat16)


def dot3(a, b):
    a_hi, a_lo = split(a)
    b_hi, b_lo = split(b)
    d = functools.partial(jnp.dot, preferred_element_type=jnp.float32)
    return d(a_hi, b_hi) + (d(a_hi, b_lo) + d(a_lo, b_hi))


def put3(dst, row0, hi, lo, rows):
    dst[row0:row0 + rows] = hi
    dst[row0 + rows:row0 + 2 * rows] = lo
    dst[row0 + 2 * rows:row0 + 3 * rows] = hi


def scale_kernel(s_ref, b_ref, o_ref, dcat):
    nb = s_ref.shape[1] // BLK
    pw = 2 * BLK

    @pl.when(pl.program_id(0) == 0)
    def _():
        zero = jnp.zeros((BLK, BLK), jnp.float32)
        for q in range(nb // 2):
            a, b = 2 * q, 2 * q + 1
            panel = jnp.concatenate(
                [jnp.concatenate([b_ref[a], zero], axis=1), jnp.concatenate([zero, b_ref[b]], axis=1)], axis=0
            )
            hi, lo = split(panel)
            put3(dcat.at[q], 0, hi, lo, pw)

    for q in range(nb // 2):
        cols = slice(q * pw, (q + 1) * pw)
        a_hi, a_lo = split(s_ref[:, cols])
        o_ref[:, cols] = jnp.dot(jnp.concatenate([a_hi, a_hi, a_lo], axis=1), dcat[q], preferred_element_type=jnp.float32)


def scale(sketch, block_inverses):
    rows, k = sketch.shape
    full = lambda shape: pl.BlockSpec(shape, lambda i: (0,) * len(shape))
    return pl.pallas_call(
        scale_kernel,
        out_shape=jax.ShapeDtypeStruct((rows, k), jnp.float32),
        grid=(rows // TM,),
        in_specs=[pl.BlockSpec((TM, k), lambda i: (i, 0)), full(block_inverses.shape)],
        out_specs=pl.BlockSpec((TM, k), lambda i: (i, 0)),
        scratch_shapes=[pltpu.VMEM((k // BLK // 2, 6 * BLK, 2 * BLK), jnp.bfloat16)],
        compiler_params=pltpu.CompilerParams(vmem_limit_bytes=48 * 1024 * 1024),
    )(sketch, block_inverses)


def solve_kernel(factor, share, idx_ref, own_ref, s_ref, slots_hbm, b_ref, f_ref, piv_ref, pbuf, pown, qcat, g, sem):
    nb = s_ref.shape[1] // BLK
    k = pbuf.shape[0]
    pw = 2 * BLK

    @pl.when(pl.program_id(0) == 0)
    def _():
        used = k - BLK

        def fetch(r, carry):
            pltpu.make_async_copy(slots_hbm.at[pl.ds(idx_ref[r], 1)], pbuf.at[pl.ds(r, 1)], sem.at[0]).start()
            return carry

        lax.fori_loop(0, used, fetch, 0, unroll=8)
        first = own_ref[0] * share
        for r in range(share):
            pltpu.make_async_copy(slots_hbm.at[pl.ds(idx_ref[first + r], 1)], pown.at[pl.ds(r, 1)], sem.at[1]).start()
        pltpu.make_async_copy(slots_hbm.at[pl.ds(0, used)], pbuf.at[pl.ds(0, used)], sem.at[0]).wait()
        pltpu.make_async_copy(slots_hbm.at[pl.ds(0, share)], pown, sem.at[1]).wait()
        piv_ref[...] = jnp.concatenate([pown[:, c, :] for c in range(nb)], axis=1)
        for j in range(1, nb):
            q = dot3(pbuf[: j * BLK, j, :] * factor, b_ref[j])
            hi, lo = split(q)
            for i in range(j):
                put3(qcat.at[:, j * BLK:(j + 1) * BLK], 3 * i * BLK, hi[i * BLK:(i + 1) * BLK], lo[i * BLK:(i + 1) * BLK], BLK)

    for p in range(nb // 2):
        a, b = 2 * p, 2 * p + 1
        cols = slice(p * pw, (p + 1) * pw)
        acc = s_ref[:, cols]
        if p > 0:
            acc = acc - jnp.dot(g[:, : 3 * p * pw], qcat[: 3 * p * pw, cols], preferred_element_type=jnp.float32)
        f_a = acc[:, :BLK]
        a_hi, a_lo = split(f_a)
        f_b = acc[:, BLK:] - jnp.dot(
            jnp.concatenate([a_hi, a_hi, a_lo], axis=1), qcat[3 * a * BLK:3 * b * BLK, b * BLK:(b + 1) * BLK], preferred_element_type=jnp.float32
        )
        f_ref[:, a * BLK:b * BLK] = f_a
        f_ref[:, b * BLK:(b + 1) * BLK] = f_b
        if p + 1 < nb // 2:
            b_hi, b_lo = split(f_b)
            g[:, 3 * a * BLK:(3 * a + 1) * BLK] = a_hi
            g[:, (3 * a + 1) * BLK:(3 * a + 2) * BLK] = a_hi
            g[:, (3 * a + 2) * BLK:(3 * a + 3) * BLK] = a_lo
            g[:, 3 * b * BLK:(3 * b + 1) * BLK] = b_hi
            g[:, (3 * b + 1) * BLK:(3 * b + 2) * BLK] = b_hi
            g[:, (3 * b + 2) * BLK:(3 * b + 3) * BLK] = b_lo


def solve(sketch, slots, idx, owner, share, block_inverses):
    rows, k = sketch.shape
    full = lambda shape: pl.BlockSpec(shape, lambda i, *_: (0,) * len(shape))
    return pl.pallas_call(
        functools.partial(solve_kernel, 1.0 / k**0.5, share),
        out_shape=(jax.ShapeDtypeStruct((rows, k), jnp.float32), jax.ShapeDtypeStruct((share, k), jnp.float32)),
        grid_spec=pltpu.PrefetchScalarGridSpec(
            num_scalar_prefetch=2,
            grid=(rows // TM,),
            in_specs=[pl.BlockSpec((TM, k), lambda i, *_: (i, 0)), pl.BlockSpec(memory_space=pl.ANY), full(block_inverses.shape)],
            out_specs=[pl.BlockSpec((TM, k), lambda i, *_: (i, 0)), full((share, k))],
            scratch_shapes=[
                pltpu.VMEM((k, k // BLK, BLK), jnp.float32),
                pltpu.VMEM((share, k // BLK, BLK), jnp.float32),
                pltpu.VMEM((3 * k, k), jnp.bfloat16),
                pltpu.VMEM((TM, 3 * k), jnp.bfloat16),
                pltpu.SemaphoreType.DMA((2,)),
            ],
        ),
        compiler_params=pltpu.CompilerParams(vmem_limit_bytes=56 * 1024 * 1024),
    )(idx, owner, sketch, slots, block_inverses)


def exchange_kernel(slab_hbm, gauss_hbm, slab_out, gauss_out, sems):
    row = lax.axis_index("row")
    partner = 1 - lax.axis_index("col")
    mesh_ids = pl.DeviceIdType.MESH
    barrier = pltpu.get_barrier_semaphore()
    pl.semaphore_signal(barrier, 1, device_id=(row, partner), device_id_type=mesh_ids)
    pl.semaphore_wait(barrier, 1)
    rows = slab_out.shape[0]
    copies = [
        pltpu.make_async_remote_copy(
            src_ref=slab_hbm.at[pl.ds(pl.multiple_of(partner * rows, rows), rows)],
            dst_ref=slab_out,
            send_sem=sems.at[0],
            recv_sem=sems.at[1],
            device_id=(row, partner),
            device_id_type=mesh_ids,
        ),
        pltpu.make_async_remote_copy(
            src_ref=gauss_hbm,
            dst_ref=gauss_out,
            send_sem=sems.at[2],
            recv_sem=sems.at[3],
            device_id=(row, partner),
            device_id_type=mesh_ids,
        ),
    ]
    for copy in copies:
        copy.start()
    for copy in copies:
        copy.wait()


def exchange(slab, gauss, rows):
    anywhere = pl.BlockSpec(memory_space=pl.ANY)
    return pl.pallas_call(
        exchange_kernel,
        out_shape=(jax.ShapeDtypeStruct((rows, slab.shape[1]), slab.dtype), jax.ShapeDtypeStruct(gauss.shape, gauss.dtype)),
        in_specs=[anywhere, anywhere],
        out_specs=[anywhere, anywhere],
        scratch_shapes=[pltpu.SemaphoreType.DMA((4,))],
        compiler_params=pltpu.CompilerParams(collective_id=0, has_side_effects=True),
    )(slab, gauss)


def on_device(slab, gauss, pivots, block_inverses):
    col_count = lax.axis_size("col")
    devices = lax.axis_size("row") * col_count
    col = lax.axis_index("col")
    owner = lax.axis_index("row") * col_count + col
    shard_rows = slab.shape[0] // col_count
    width = gauss.shape[1]
    swap = [(0, 1), (1, 0)]

    order = jnp.arange(pivots.shape[0], dtype=jnp.int32)
    block_of = pivots // shard_rows
    same = (block_of[:, None] == block_of[None, :]) & (order[None, :] < order[:, None])
    rank = jnp.sum(same.astype(jnp.int32), axis=1)
    local = pivots - block_of * shard_rows
    partner = owner + 1 - 2 * col
    targets = jnp.concatenate([jnp.full((SLOTS,), owner), jnp.full((SLOTS,), partner)])
    offsets = jnp.concatenate([jnp.full((SLOTS,), col), jnp.full((SLOTS,), 1 - col)]) * shard_rows
    slot_ids = jnp.concatenate([jnp.arange(SLOTS), jnp.arange(SLOTS)])
    hit = (block_of[None, :] == targets[:, None]) & (rank[None, :] == slot_ids[:, None])
    where_row = jnp.sum(jnp.where(hit, local[None, :], 0), axis=1) + offsets
    pick = where_row[:, None] == jnp.arange(slab.shape[0], dtype=jnp.int32)[None, :]
    rows = jnp.dot(pick.astype(slab.dtype), slab, preferred_element_type=jnp.float32).astype(slab.dtype)
    parts = jnp.dot(rows, gauss, preferred_element_type=jnp.float32)
    own_slots = parts[:SLOTS] + lax.ppermute(parts[SLOTS:], "col", swap)
    slots = lax.all_gather(own_slots.reshape(SLOTS, width // BLK, BLK), ("row", "col"), tiled=True)

    mine = lax.dynamic_slice_in_dim(slab, col * shard_rows, shard_rows, 0)
    other_slab, other_gauss = exchange(slab, gauss, shard_rows)
    sketch = jnp.dot(mine, gauss, preferred_element_type=jnp.float32) + jnp.dot(
        other_slab, other_gauss, preferred_element_type=jnp.float32
    )

    share = width // devices
    scaled = scale(sketch, block_inverses)
    factor_rows, own_pivots = solve(scaled, slots, block_of * SLOTS + rank, owner[None], share, block_inverses)
    return (factor_rows, own_pivots)


def solution(mesh):
    return jax.shard_map(
        on_device,
        mesh=mesh,
        in_specs=(P("row", "col"), P("col", None), P(), P()),
        out_specs=(P(("row", "col"), None), P(("row", "col"), None)),
        check_vma=False,
    )
```

```python
import functools

import jax
import jax.numpy as jnp
from jax import lax
from jax.experimental import pallas as pl
from jax.experimental.pallas import tpu as pltpu
from jax.sharding import PartitionSpec as P

K = 1024
BLK = 128
SLOTS = 32
TM = 1024


def split(x):
    hi = x.astype(jnp.bfloat16)
    return hi, (x - hi.astype(jnp.float32)).astype(jnp.bfloat16)


def dot3(a, b):
    a_hi, a_lo = split(a)
    b_hi, b_lo = split(b)
    d = functools.partial(jnp.dot, preferred_element_type=jnp.float32)
    return d(a_hi, b_hi) + (d(a_hi, b_lo) + d(a_lo, b_hi))


def put3(dst, row0, hi, lo, rows):
    dst[row0:row0 + rows] = hi
    dst[row0 + rows:row0 + 2 * rows] = lo
    dst[row0 + 2 * rows:row0 + 3 * rows] = hi


def scale_kernel(s_ref, b_ref, o_ref, dcat):
    nb = s_ref.shape[1] // BLK
    pw = 2 * BLK

    @pl.when(pl.program_id(0) == 0)
    def _():
        zero = jnp.zeros((BLK, BLK), jnp.float32)
        for q in range(nb // 2):
            a, b = 2 * q, 2 * q + 1
            panel = jnp.concatenate(
                [jnp.concatenate([b_ref[a], zero], axis=1), jnp.concatenate([zero, b_ref[b]], axis=1)], axis=0
            )
            hi, lo = split(panel)
            put3(dcat.at[q], 0, hi, lo, pw)

    for q in range(nb // 2):
        cols = slice(q * pw, (q + 1) * pw)
        a_hi, a_lo = split(s_ref[:, cols])
        o_ref[:, cols] = jnp.dot(jnp.concatenate([a_hi, a_hi, a_lo], axis=1), dcat[q], preferred_element_type=jnp.float32)


def scale(sketch, block_inverses):
    rows, k = sketch.shape
    full = lambda shape: pl.BlockSpec(shape, lambda i: (0,) * len(shape))
    return pl.pallas_call(
        scale_kernel,
        out_shape=jax.ShapeDtypeStruct((rows, k), jnp.float32),
        grid=(rows // TM,),
        in_specs=[pl.BlockSpec((TM, k), lambda i: (i, 0)), full(block_inverses.shape)],
        out_specs=pl.BlockSpec((TM, k), lambda i: (i, 0)),
        scratch_shapes=[pltpu.VMEM((k // BLK // 2, 6 * BLK, 2 * BLK), jnp.bfloat16)],
        compiler_params=pltpu.CompilerParams(vmem_limit_bytes=48 * 1024 * 1024),
    )(sketch, block_inverses)


def solve_kernel(factor, share, idx_ref, own_ref, s_ref, slots_hbm, b_ref, f_ref, piv_ref, pbuf, qcat, g, sem):
    nb = s_ref.shape[1] // BLK
    k = pbuf.shape[0]
    pw = 2 * BLK

    @pl.when(pl.program_id(0) == 0)
    def _():
        used = k - BLK

        def fetch(r, carry):
            pltpu.make_async_copy(slots_hbm.at[pl.ds(idx_ref[r], 1)], pbuf.at[pl.ds(r, 1)], sem.at[0]).start()
            return carry

        lax.fori_loop(0, used, fetch, 0, unroll=32)
        first = own_ref[0] * share
        for r in range(share):
            pltpu.make_async_copy(slots_hbm.at[pl.ds(idx_ref[first + r], 1)], piv_ref.at[pl.ds(r, 1)], sem.at[1]).start()
        pltpu.make_async_copy(slots_hbm.at[pl.ds(0, used)], pbuf.at[pl.ds(0, used)], sem.at[0]).wait()
        pltpu.make_async_copy(slots_hbm.at[pl.ds(0, share)], piv_ref, sem.at[1]).wait()
        for j in range(1, nb):
            q = dot3(pbuf[: j * BLK, j * BLK:(j + 1) * BLK] * factor, b_ref[j])
            hi, lo = split(q)
            for i in range(j):
                put3(qcat.at[:, j * BLK:(j + 1) * BLK], 3 * i * BLK, hi[i * BLK:(i + 1) * BLK], lo[i * BLK:(i + 1) * BLK], BLK)

    for p in range(nb // 2):
        a, b = 2 * p, 2 * p + 1
        cols = slice(p * pw, (p + 1) * pw)
        acc = s_ref[:, cols]
        if p > 0:
            acc = acc - jnp.dot(g[:, : 3 * p * pw], qcat[: 3 * p * pw, cols], preferred_element_type=jnp.float32)
        f_a = acc[:, :BLK]
        a_hi, a_lo = split(f_a)
        f_b = acc[:, BLK:] - jnp.dot(
            jnp.concatenate([a_hi, a_hi, a_lo], axis=1), qcat[3 * a * BLK:3 * b * BLK, b * BLK:(b + 1) * BLK], preferred_element_type=jnp.float32
        )
        f_ref[:, a * BLK:b * BLK] = f_a
        f_ref[:, b * BLK:(b + 1) * BLK] = f_b
        if p + 1 < nb // 2:
            b_hi, b_lo = split(f_b)
            g[:, 3 * a * BLK:(3 * a + 1) * BLK] = a_hi
            g[:, (3 * a + 1) * BLK:(3 * a + 2) * BLK] = a_hi
            g[:, (3 * a + 2) * BLK:(3 * a + 3) * BLK] = a_lo
            g[:, 3 * b * BLK:(3 * b + 1) * BLK] = b_hi
            g[:, (3 * b + 1) * BLK:(3 * b + 2) * BLK] = b_hi
            g[:, (3 * b + 2) * BLK:(3 * b + 3) * BLK] = b_lo


def solve(sketch, slots, idx, owner, share, block_inverses):
    rows, k = sketch.shape
    full = lambda shape: pl.BlockSpec(shape, lambda i, *_: (0,) * len(shape))
    return pl.pallas_call(
        functools.partial(solve_kernel, 1.0 / k**0.5, share),
        out_shape=(jax.ShapeDtypeStruct((rows, k), jnp.float32), jax.ShapeDtypeStruct((share, k), jnp.float32)),
        grid_spec=pltpu.PrefetchScalarGridSpec(
            num_scalar_prefetch=2,
            grid=(rows // TM,),
            in_specs=[pl.BlockSpec((TM, k), lambda i, *_: (i, 0)), pl.BlockSpec(memory_space=pl.ANY), full(block_inverses.shape)],
            out_specs=[pl.BlockSpec((TM, k), lambda i, *_: (i, 0)), full((share, k))],
            scratch_shapes=[
                pltpu.VMEM((k, k), jnp.float32),
                pltpu.VMEM((3 * k, k), jnp.bfloat16),
                pltpu.VMEM((TM, 3 * k), jnp.bfloat16),
                pltpu.SemaphoreType.DMA((2,)),
            ],
        ),
        compiler_params=pltpu.CompilerParams(vmem_limit_bytes=56 * 1024 * 1024),
    )(idx, owner, sketch, slots, block_inverses)


def exchange_kernel(slab_hbm, gauss_hbm, slab_out, gauss_out, sems):
    row = lax.axis_index("row")
    partner = 1 - lax.axis_index("col")
    mesh_ids = pl.DeviceIdType.MESH
    barrier = pltpu.get_barrier_semaphore()
    pl.semaphore_signal(barrier, 1, device_id=(row, partner), device_id_type=mesh_ids)
    pl.semaphore_wait(barrier, 1)
    rows = slab_out.shape[0]
    copies = [
        pltpu.make_async_remote_copy(
            src_ref=slab_hbm.at[pl.ds(pl.multiple_of(partner * rows, rows), rows)],
            dst_ref=slab_out,
            send_sem=sems.at[0],
            recv_sem=sems.at[1],
            device_id=(row, partner),
            device_id_type=mesh_ids,
        ),
        pltpu.make_async_remote_copy(
            src_ref=gauss_hbm,
            dst_ref=gauss_out,
            send_sem=sems.at[2],
            recv_sem=sems.at[3],
            device_id=(row, partner),
            device_id_type=mesh_ids,
        ),
    ]
    for copy in copies:
        copy.start()
    for copy in copies:
        copy.wait()


def exchange(slab, gauss, rows):
    anywhere = pl.BlockSpec(memory_space=pl.ANY)
    return pl.pallas_call(
        exchange_kernel,
        out_shape=(jax.ShapeDtypeStruct((rows, slab.shape[1]), slab.dtype), jax.ShapeDtypeStruct(gauss.shape, gauss.dtype)),
        in_specs=[anywhere, anywhere],
        out_specs=[anywhere, anywhere],
        scratch_shapes=[pltpu.SemaphoreType.DMA((4,))],
        compiler_params=pltpu.CompilerParams(collective_id=0, has_side_effects=True),
    )(slab, gauss)


def on_device(slab, gauss, pivots, block_inverses):
    col_count = lax.axis_size("col")
    devices = lax.axis_size("row") * col_count
    col = lax.axis_index("col")
    owner = lax.axis_index("row") * col_count + col
    shard_rows = slab.shape[0] // col_count
    width = gauss.shape[1]
    swap = [(0, 1), (1, 0)]

    order = jnp.arange(pivots.shape[0], dtype=jnp.int32)
    block_of = pivots // shard_rows
    same = (block_of[:, None] == block_of[None, :]) & (order[None, :] < order[:, None])
    rank = jnp.sum(same.astype(jnp.int32), axis=1)
    local = pivots - block_of * shard_rows
    partner = owner + 1 - 2 * col
    targets = jnp.concatenate([jnp.full((SLOTS,), owner), jnp.full((SLOTS,), partner)])
    offsets = jnp.concatenate([jnp.full((SLOTS,), col), jnp.full((SLOTS,), 1 - col)]) * shard_rows
    slot_ids = jnp.concatenate([jnp.arange(SLOTS), jnp.arange(SLOTS)])
    hit = (block_of[None, :] == targets[:, None]) & (rank[None, :] == slot_ids[:, None])
    where_row = jnp.sum(jnp.where(hit, local[None, :], 0), axis=1) + offsets
    pick = where_row[:, None] == jnp.arange(slab.shape[0], dtype=jnp.int32)[None, :]
    rows = jnp.dot(pick.astype(slab.dtype), slab, preferred_element_type=jnp.float32).astype(slab.dtype)
    parts = jnp.dot(rows, gauss, preferred_element_type=jnp.float32)
    own_slots = parts[:SLOTS] + lax.ppermute(parts[SLOTS:], "col", swap)
    slots = lax.all_gather(own_slots, ("row", "col"), tiled=True)

    mine = lax.dynamic_slice_in_dim(slab, col * shard_rows, shard_rows, 0)
    other_slab, other_gauss = exchange(slab, gauss, shard_rows)
    sketch = jnp.dot(mine, gauss, preferred_element_type=jnp.float32) + jnp.dot(
        other_slab, other_gauss, preferred_element_type=jnp.float32
    )

    share = width // devices
    scaled = scale(sketch, block_inverses)
    factor_rows, own_pivots = solve(scaled, slots, block_of * SLOTS + rank, owner[None], share, block_inverses)
    return (factor_rows, own_pivots)


def solution(mesh):
    return jax.shard_map(
        on_device,
        mesh=mesh,
        in_specs=(P("row", "col"), P("col", None), P(), P()),
        out_specs=(P(("row", "col"), None), P(("row", "col"), None)),
        check_vma=False,
    )
```

```python
import functools

import jax
import jax.numpy as jnp
from jax import lax
from jax.experimental import pallas as pl
from jax.experimental.pallas import tpu as pltpu
from jax.sharding import PartitionSpec as P

K = 1024
BLK = 128
SLOTS = 32
TM = 1024


def split(x):
    hi = x.astype(jnp.bfloat16)
    return hi, (x - hi.astype(jnp.float32)).astype(jnp.bfloat16)


def dot3(a, b):
    a_hi, a_lo = split(a)
    b_hi, b_lo = split(b)
    d = functools.partial(jnp.dot, preferred_element_type=jnp.float32)
    return d(a_hi, b_hi) + (d(a_hi, b_lo) + d(a_lo, b_hi))


def put3(dst, row0, hi, lo, rows):
    dst[row0:row0 + rows] = hi
    dst[row0 + rows:row0 + 2 * rows] = lo
    dst[row0 + 2 * rows:row0 + 3 * rows] = hi


def scale_kernel(s_ref, b_ref, o_ref, dcat):
    nb = s_ref.shape[1] // BLK
    pw = 2 * BLK

    @pl.when(pl.program_id(0) == 0)
    def _():
        zero = jnp.zeros((BLK, BLK), jnp.float32)
        for q in range(nb // 2):
            a, b = 2 * q, 2 * q + 1
            panel = jnp.concatenate(
                [jnp.concatenate([b_ref[a], zero], axis=1), jnp.concatenate([zero, b_ref[b]], axis=1)], axis=0
            )
            hi, lo = split(panel)
            put3(dcat.at[q], 0, hi, lo, pw)

    for q in range(nb // 2):
        cols = slice(q * pw, (q + 1) * pw)
        a_hi, a_lo = split(s_ref[:, cols])
        o_ref[:, cols] = jnp.dot(jnp.concatenate([a_hi, a_hi, a_lo], axis=1), dcat[q], preferred_element_type=jnp.float32)


def scale(sketch, block_inverses):
    rows, k = sketch.shape
    full = lambda shape: pl.BlockSpec(shape, lambda i: (0,) * len(shape))
    return pl.pallas_call(
        scale_kernel,
        out_shape=jax.ShapeDtypeStruct((rows, k), jnp.float32),
        grid=(rows // TM,),
        in_specs=[pl.BlockSpec((TM, k), lambda i: (i, 0)), full(block_inverses.shape)],
        out_specs=pl.BlockSpec((TM, k), lambda i: (i, 0)),
        scratch_shapes=[pltpu.VMEM((k // BLK // 2, 6 * BLK, 2 * BLK), jnp.bfloat16)],
        compiler_params=pltpu.CompilerParams(vmem_limit_bytes=48 * 1024 * 1024),
    )(sketch, block_inverses)


def solve_kernel(factor, share, idx_ref, own_ref, s_ref, slots_hbm, b_ref, f_ref, piv_ref, pbuf, qcat, g, sem):
    nb = s_ref.shape[1] // BLK
    k = pbuf.shape[0]
    pw = 2 * BLK

    @pl.when(pl.program_id(0) == 0)
    def _():
        used = k - BLK

        def fetch(r, carry):
            pltpu.make_async_copy(slots_hbm.at[pl.ds(idx_ref[r], 1)], pbuf.at[pl.ds(r, 1)], sem.at[0]).start()
            return carry

        lax.fori_loop(0, used, fetch, 0, unroll=32)
        first = own_ref[0] * share
        for r in range(share):
            pltpu.make_async_copy(slots_hbm.at[pl.ds(idx_ref[first + r], 1)], piv_ref.at[pl.ds(r, 1)], sem.at[1]).start()
        pltpu.make_async_copy(slots_hbm.at[pl.ds(0, used)], pbuf.at[pl.ds(0, used)], sem.at[0]).wait()
        pltpu.make_async_copy(slots_hbm.at[pl.ds(0, share)], piv_ref, sem.at[1]).wait()
        for j in range(1, nb):
            q = dot3(pbuf[: j * BLK, j * BLK:(j + 1) * BLK] * factor, b_ref[j])
            hi, lo = split(q)
            for i in range(j):
                put3(qcat.at[:, j * BLK:(j + 1) * BLK], 3 * i * BLK, hi[i * BLK:(i + 1) * BLK], lo[i * BLK:(i + 1) * BLK], BLK)

    for p in range(nb // 2):
        a, b = 2 * p, 2 * p + 1
        cols = slice(p * pw, (p + 1) * pw)
        acc = s_ref[:, cols]
        if p > 0:
            acc = acc - jnp.dot(g[:, : 3 * p * pw], qcat[: 3 * p * pw, cols], preferred_element_type=jnp.float32)
        f_a = acc[:, :BLK]
        a_hi, a_lo = split(f_a)
        f_b = acc[:, BLK:] - jnp.dot(
            jnp.concatenate([a_hi, a_hi, a_lo], axis=1), qcat[3 * a * BLK:3 * b * BLK, b * BLK:(b + 1) * BLK], preferred_element_type=jnp.float32
        )
        f_ref[:, a * BLK:b * BLK] = f_a
        f_ref[:, b * BLK:(b + 1) * BLK] = f_b
        if p + 1 < nb // 2:
            b_hi, b_lo = split(f_b)
            g[:, 3 * a * BLK:(3 * a + 1) * BLK] = a_hi
            g[:, (3 * a + 1) * BLK:(3 * a + 2) * BLK] = a_hi
            g[:, (3 * a + 2) * BLK:(3 * a + 3) * BLK] = a_lo
            g[:, 3 * b * BLK:(3 * b + 1) * BLK] = b_hi
            g[:, (3 * b + 1) * BLK:(3 * b + 2) * BLK] = b_hi
            g[:, (3 * b + 2) * BLK:(3 * b + 3) * BLK] = b_lo


def solve(sketch, slots, idx, owner, share, block_inverses):
    rows, k = sketch.shape
    full = lambda shape: pl.BlockSpec(shape, lambda i, *_: (0,) * len(shape))
    return pl.pallas_call(
        functools.partial(solve_kernel, 1.0 / k**0.5, share),
        out_shape=(jax.ShapeDtypeStruct((rows, k), jnp.float32), jax.ShapeDtypeStruct((share, k), jnp.float32)),
        grid_spec=pltpu.PrefetchScalarGridSpec(
            num_scalar_prefetch=2,
            grid=(rows // TM,),
            in_specs=[pl.BlockSpec((TM, k), lambda i, *_: (i, 0)), pl.BlockSpec(memory_space=pl.ANY), full(block_inverses.shape)],
            out_specs=[pl.BlockSpec((TM, k), lambda i, *_: (i, 0)), full((share, k))],
            scratch_shapes=[
                pltpu.VMEM((k, k), jnp.float32),
                pltpu.VMEM((3 * k, k), jnp.bfloat16),
                pltpu.VMEM((TM, 3 * k), jnp.bfloat16),
                pltpu.SemaphoreType.DMA((2,)),
            ],
        ),
        compiler_params=pltpu.CompilerParams(vmem_limit_bytes=56 * 1024 * 1024),
    )(idx, owner, sketch, slots, block_inverses)


def exchange_kernel(slab_hbm, gauss_hbm, slab_out, gauss_out, sems):
    row = lax.axis_index("row")
    partner = 1 - lax.axis_index("col")
    mesh_ids = pl.DeviceIdType.MESH
    barrier = pltpu.get_barrier_semaphore()
    pl.semaphore_signal(barrier, 1, device_id=(row, partner), device_id_type=mesh_ids)
    pl.semaphore_wait(barrier, 1)
    rows = slab_out.shape[0]
    copies = [
        pltpu.make_async_remote_copy(
            src_ref=slab_hbm.at[pl.ds(pl.multiple_of(partner * rows, rows), rows)],
            dst_ref=slab_out,
            send_sem=sems.at[0],
            recv_sem=sems.at[1],
            device_id=(row, partner),
            device_id_type=mesh_ids,
        ),
        pltpu.make_async_remote_copy(
            src_ref=gauss_hbm,
            dst_ref=gauss_out,
            send_sem=sems.at[2],
            recv_sem=sems.at[3],
            device_id=(row, partner),
            device_id_type=mesh_ids,
        ),
    ]
    for copy in copies:
        copy.start()
    for copy in copies:
        copy.wait()


def exchange(slab, gauss, rows):
    anywhere = pl.BlockSpec(memory_space=pl.ANY)
    return pl.pallas_call(
        exchange_kernel,
        out_shape=(jax.ShapeDtypeStruct((rows, slab.shape[1]), slab.dtype), jax.ShapeDtypeStruct(gauss.shape, gauss.dtype)),
        in_specs=[anywhere, anywhere],
        out_specs=[anywhere, anywhere],
        scratch_shapes=[pltpu.SemaphoreType.DMA((4,))],
        compiler_params=pltpu.CompilerParams(collective_id=0, has_side_effects=True),
    )(slab, gauss)


def on_device(slab, gauss, pivots, block_inverses):
    col_count = lax.axis_size("col")
    devices = lax.axis_size("row") * col_count
    col = lax.axis_index("col")
    owner = lax.axis_index("row") * col_count + col
    shard_rows = slab.shape[0] // col_count
    width = gauss.shape[1]
    swap = [(0, 1), (1, 0)]

    order = jnp.arange(pivots.shape[0], dtype=jnp.int32)
    block_of = pivots // shard_rows
    same = (block_of[:, None] == block_of[None, :]) & (order[None, :] < order[:, None])
    rank = jnp.sum(same.astype(jnp.int32), axis=1)
    local = pivots - block_of * shard_rows
    partner = owner + 1 - 2 * col
    targets = jnp.concatenate([jnp.full((SLOTS,), owner), jnp.full((SLOTS,), partner)])
    offsets = jnp.concatenate([jnp.full((SLOTS,), col), jnp.full((SLOTS,), 1 - col)]) * shard_rows
    slot_ids = jnp.concatenate([jnp.arange(SLOTS), jnp.arange(SLOTS)])
    in_target = (block_of[None, :] == jnp.stack([owner, partner])[:, None]).astype(jnp.bfloat16)
    before = (order[:, None] < order[None, :]).astype(jnp.bfloat16)
    count = jnp.dot(in_target, before, preferred_element_type=jnp.float32).astype(jnp.int32)
    counts = jnp.concatenate([jnp.broadcast_to(count[0], (SLOTS, count.shape[1])), jnp.broadcast_to(count[1], (SLOTS, count.shape[1]))])
    hit = (block_of[None, :] == targets[:, None]) & (counts == slot_ids[:, None])
    where_row = jnp.sum(jnp.where(hit, local[None, :], 0), axis=1) + offsets
    pick = where_row[:, None] == jnp.arange(slab.shape[0], dtype=jnp.int32)[None, :]
    rows = jnp.dot(pick.astype(slab.dtype), slab, preferred_element_type=jnp.float32).astype(slab.dtype)
    parts = jnp.dot(rows, gauss, preferred_element_type=jnp.float32)
    own_slots = parts[:SLOTS] + lax.ppermute(parts[SLOTS:], "col", swap)
    slots = lax.all_gather(own_slots, ("row", "col"), tiled=True)

    mine = lax.dynamic_slice_in_dim(slab, col * shard_rows, shard_rows, 0)
    other_slab, other_gauss = exchange(slab, gauss, shard_rows)
    sketch = jnp.dot(mine, gauss, preferred_element_type=jnp.float32) + jnp.dot(
        other_slab, other_gauss, preferred_element_type=jnp.float32
    )

    share = width // devices
    scaled = scale(sketch, block_inverses)
    factor_rows, own_pivots = solve(scaled, slots, block_of * SLOTS + rank, owner[None], share, block_inverses)
    return (factor_rows, own_pivots)


def solution(mesh):
    return jax.shard_map(
        on_device,
        mesh=mesh,
        in_specs=(P("row", "col"), P("col", None), P(), P()),
        out_specs=(P(("row", "col"), None), P(("row", "col"), None)),
        check_vma=False,
    )
```
